32 devices in a mesh: pts: 8 (over z, y), grp: 4 (over x, core).
Axes of the slice: x: 2, y: 2, z: 4, core: 2. Of those that a mesh axis runs over, the one named last changes fastest.
Arguments:
- jacobian: bfloat16 [32, 6, 128, 3, 256], P(('pts', 'grp')), may hold values from -0.21875 to 0.21875
- point_blocks: float32 [32, 6, 256], P(('pts', 'grp')), may hold values from -0.5 to 4, as said below
- point_grad: bfloat16 [32, 3, 256], P(('pts', 'grp')), may hold values from -6 to 6
- camera_grad: float32 [32, 128], P(('pts', 'grp')), may hold values from -6 to 6
- damping: float32 [32, 128], replicated, may hold values from 1 to 8
- incidence: int32 [32, 6], P(('pts', 'grp')), may hold values from 0 to 31, as said below
- tile_owner: int32 [8], replicated, may hold values from 0 to 7, each once
- front_first: int32 [1], replicated, may hold values from 0 to 31
Outputs:
- tiles_out: float32 [256, 128, 128], P(('pts', 'grp'))
- rhs_out: float32 [32, 128], P(('pts', 'grp'))
- front_panel: float32 [2304, 512], P(None, 'grp')
The draws below stay inside these ranges and needn't reach their ends.
Inputs may be any that keep to these rules, and one draw needn't show every extreme that they name: `incidence`: point cluster p names 6 different camera clusters, all among (p + t) mod 32 for t from 0 to 7. `point_blocks`: each point's diagonal entries exceed the sum of the magnitudes of the two off-diagonal entries of their row by 0.1 or more. `tile_owner`: A permutation of the pts indices.
All inputs are finite; a program needn't handle non-finite values.
Results may differ from the reference program's by a relative error of at most 0.0022.
Values sent between devices are 32-bit elements; how exact they have to be, the bound alone decides.
No kernel may reach another device: no remote copies, remote signals or barrier semaphores. Data moves between devices by JAX's collectives and lax.ppermute only.
A program may use at most 128 MiB of HBM per device.

```python
import math
import jax
import jax.numpy as jnp
import numpy as np
from jax import lax

CR = 128
PTS = 256
TOUCH = 6
BAND = 8
FRONT = 4
PC_DEV = 1
NC = 32
NPC = 32
WIN = 18
N_PTS = 8
N_GRP = 4


def draw_incidence(key, part):
    scores = jax.random.randint(key, (NPC, BAND), 0, 1 << 20) * BAND + jnp.arange(BAND)[None, :]
    ordering = jnp.argsort(scores, axis=1)
    chosen = ordering[:, :TOUCH].astype(jnp.int32)
    owners = (jnp.arange(NPC) // PC_DEV).astype(jnp.int32)
    return jnp.mod(owners[:, None] + chosen, NC).astype(jnp.int32)


def draw_point_blocks(key, part):
    key_diag, key_cross = jax.random.split(jax.random.fold_in(key, 7))
    diagonal = jax.random.uniform(key_diag, (NPC, 3, PTS), jnp.float32, 1.5, 3.0)
    crossed = jax.random.uniform(key_cross, (NPC, 3, PTS), jnp.float32, -0.5, 0.5)
    return jnp.concatenate([diagonal, crossed], axis=1).astype(jnp.float32)


def shard_levels(key, extent, shards, least, largest):
    def one(dim, blocks):
        heights = jax.random.uniform(jax.random.fold_in(jax.random.fold_in(key, 6), dim), (blocks,), jnp.float32, least / len(shards), largest / len(shards))
        return jnp.repeat(jnp.exp(heights), extent[dim] // blocks).reshape((-1,) + (1,) * (len(extent) - dim - 1))

    level = one(*shards[0])
    for cut in shards[1:]:
        level = level * one(*cut)
    return level


def normal_values(rng, shape, scale, most, cuts=(), kind=jnp.bfloat16):
    values = scale * jax.random.normal(rng, shape, jnp.float32)
    if cuts:
        values = values * shard_levels(rng, shape, cuts, -0.22, 0.18)
    return jnp.clip(values, -most, most).astype(kind)


def setup_inputs(seed: int = 0) -> dict:
    splits = jax.random.split(jax.random.key(seed), 9)
    return {
        "jacobian": normal_values(splits[0], (NPC, TOUCH, CR, 3, PTS), (3 * PTS) ** -0.5, 0.21875, ((0, 32),)),
        "point_blocks": draw_point_blocks(jax.random.fold_in(splits[8], 71), 0),
        "point_grad": normal_values(splits[2], (NPC, 3, PTS), 1.0, 6.0, ((0, 32),)),
        "camera_grad": normal_values(splits[3], (NC, CR), 1.0, 6.0, ((0, 32),), jnp.float32),
        "damping": jnp.clip(jnp.exp(jax.random.uniform(splits[4], (NC, CR), jnp.float32, math.log(1.0), math.log(8.0))), 1.0, 8.0),
        "incidence": draw_incidence(jax.random.fold_in(splits[8], 71), 0),
        "tile_owner": jax.random.permutation(splits[6], N_PTS).astype(jnp.int32),
        "front_first": jax.random.randint(splits[7], (1,), 0, NC).astype(jnp.int32),
    }


PRECISE = lax.Precision.HIGHEST

def invert_blocks(blocks):
    diag_x = blocks[:, 0]
    diag_y = blocks[:, 1]
    diag_z = blocks[:, 2]
    cross_xy = blocks[:, 3]
    cross_xz = blocks[:, 4]
    cross_yz = blocks[:, 5]
    adj_xx = diag_y * diag_z - cross_yz * cross_yz
    adj_yy = diag_x * diag_z - cross_xz * cross_xz
    adj_zz = diag_x * diag_y - cross_xy * cross_xy
    adj_xy = cross_xz * cross_yz - cross_xy * diag_z
    adj_xz = cross_xy * cross_yz - diag_y * cross_xz
    adj_yz = cross_xy * cross_xz - diag_x * cross_yz
    determinant = diag_x * adj_xx + cross_xy * adj_xy + cross_xz * adj_xz
    inverse_det = 1.0 / determinant
    return [[adj_xx * inverse_det, adj_xy * inverse_det, adj_xz * inverse_det], [adj_xy * inverse_det, adj_yy * inverse_det, adj_yz * inverse_det], [adj_xz * inverse_det, adj_yz * inverse_det, adj_zz * inverse_det]]

def scale_jacobian(jacobian, blocks):
    inverse = invert_blocks(blocks)
    widened = jacobian.astype(jnp.float32)
    columns = []
    for target in range(3):
        summed = widened[:, :, :, 0, :] * inverse[0][target][:, None, None, :]
        summed = summed + widened[:, :, :, 1, :] * inverse[1][target][:, None, None, :]
        summed = summed + widened[:, :, :, 2, :] * inverse[2][target][:, None, None, :]
        columns.append(summed)
    return jnp.stack(columns, axis=3).astype(jnp.bfloat16)

def reference(jacobian, point_blocks, point_grad, camera_grad, damping, incidence, tile_owner, front_first):
    clusters = N_PTS * N_GRP
    point_cols = 3 * PTS
    grouped_jac = jacobian.reshape(clusters, PC_DEV, TOUCH, CR, 3, PTS)
    grouped_blocks = point_blocks.reshape(clusters, PC_DEV, 6, PTS)
    grouped_grad = point_grad.reshape(clusters, PC_DEV, 3, PTS)
    grouped_inc = incidence.reshape(clusters, PC_DEV, TOUCH)
    row_axis = np.arange(BAND)[:, None]
    take_cols = np.minimum(row_axis + np.arange(BAND)[None, :], BAND - 1)
    keep_band = jnp.asarray(row_axis + np.arange(BAND)[None, :] <= BAND - 1, jnp.float32)

    def advance(carry, inputs):
        tiles_window, rhs_window = carry
        device, jac_blk, blocks_blk, grad_blk, inc_blk = inputs
        scaled = scale_jacobian(jac_blk, blocks_blk)
        scaled_flat = scaled.reshape(PC_DEV, TOUCH, CR, point_cols).astype(jnp.float32)
        jac_flat = jac_blk.reshape(PC_DEV, TOUCH, CR, point_cols).astype(jnp.float32)
        pair_blocks = jnp.einsum('pkrx,plcx->pkrlc', scaled_flat, jac_flat, precision=PRECISE)
        pulled = jnp.einsum('pkrx,px->pkr', scaled_flat, grad_blk.reshape(PC_DEV, point_cols).astype(jnp.float32), precision=PRECISE)
        local_slot = jnp.mod(inc_blk - device, clusters)
        placing = (local_slot[:, None, :] == jnp.arange(BAND)[None, :, None]).astype(jnp.float32)
        spread = jnp.einsum('ptk,pkrlc->ptrlc', placing, pair_blocks, precision=PRECISE)
        band_grid = jnp.einsum('pql,ptrlc->tqrc', placing, spread, precision=PRECISE)
        tiles_window = tiles_window + band_grid[row_axis, take_cols] * keep_band[:, :, None, None]
        rhs_window = rhs_window + jnp.einsum('ptk,pkr->tr', placing, pulled, precision=PRECISE)
        emitted = (tiles_window[0], rhs_window[0])
        tiles_window = jnp.concatenate([tiles_window[1:], jnp.zeros((1, BAND, CR, CR), jnp.float32)], axis=0)
        rhs_window = jnp.concatenate([rhs_window[1:], jnp.zeros((1, CR), jnp.float32)], axis=0)
        return ((tiles_window, rhs_window), emitted)
    start_carry = (jnp.zeros((BAND, BAND, CR, CR), jnp.float32), jnp.zeros((BAND, CR), jnp.float32))
    devices = jnp.arange(clusters, dtype=jnp.int32)
    final_carry, emitted = lax.scan(advance, start_carry, (devices, grouped_jac, grouped_blocks, grouped_grad, grouped_inc))
    tile_rows, rhs_rows = emitted
    tile_rows = tile_rows.at[:BAND - 1].add(final_carry[0][:BAND - 1])
    rhs_rows = rhs_rows.at[:BAND - 1].add(final_carry[1][:BAND - 1])
    identity = jnp.eye(CR, dtype=jnp.float32)
    tile_rows = tile_rows.at[:, 0].add(damping[:, :, None] * identity[None, :, :])
    schur = tile_rows.reshape(BAND * clusters, CR, CR)
    reduced = camera_grad - rhs_rows
    front_start = front_first[0]
    window_base = front_start - (BAND - 1)
    row_blocks = []
    for position in range(WIN):
        member = jnp.mod(window_base + position, clusters)
        entries = []
        for front_pos in range(FRONT):
            front_id = jnp.mod(front_start + front_pos, clusters)
            ahead = jnp.mod(front_id - member, clusters)
            behind = jnp.mod(member - front_id, clusters)
            tile_fwd = schur[BAND * member + jnp.minimum(ahead, BAND - 1)]
            tile_back = schur[BAND * front_id + jnp.minimum(behind, BAND - 1)].T
            entries.append(jnp.where(ahead < BAND, tile_fwd, jnp.where(behind < BAND, tile_back, 0.0)))
        row_blocks.append(jnp.concatenate(entries, axis=1))
    window_columns = jnp.concatenate(row_blocks, axis=0)
    square = window_columns[(BAND - 1) * CR:(BAND - 1 + FRONT) * CR]
    factor = jnp.linalg.cholesky(square)
    front_panel = jax.scipy.linalg.solve_triangular(factor, window_columns.T, lower=True).T
    panel_blocks = front_panel.reshape(WIN, CR, FRONT * CR)

    def outside_front(position):
        return position < BAND - 1 or position >= BAND - 1 + FRONT
    for position in range(WIN):
        for offset in range(BAND):
            partner = position + offset
            if partner < WIN and outside_front(position) and outside_front(partner):
                member = jnp.mod(window_base + position, clusters)
                change = jnp.dot(panel_blocks[position], panel_blocks[partner].T, precision=PRECISE)
                schur = schur.at[BAND * member + offset].add(-change)
    front_ids = jnp.mod(front_start + jnp.arange(FRONT), clusters)
    solved_front = jax.scipy.linalg.solve_triangular(factor, reduced[front_ids].reshape(FRONT * CR), lower=True)
    rhs_out = reduced
    for position in range(WIN):
        member = jnp.mod(window_base + position, clusters)
        if outside_front(position):
            rhs_out = rhs_out.at[member].set(reduced[member] - jnp.dot(panel_blocks[position], solved_front, precision=PRECISE))
        else:
            front_pos = position - (BAND - 1)
            rhs_out = rhs_out.at[member].set(solved_front[front_pos * CR:(front_pos + 1) * CR])
    per_owner = BAND * clusters // N_PTS
    perm_inverse = jnp.zeros((N_PTS,), jnp.int32).at[tile_owner].set(jnp.arange(N_PTS, dtype=jnp.int32))
    arranged = schur.reshape(per_owner, N_PTS, CR, CR).transpose(1, 0, 2, 3)[perm_inverse]
    tiles_out = arranged.reshape(BAND * clusters, CR, CR)
    return (tiles_out, rhs_out, front_panel)
```

```python
import functools

import jax
import jax.numpy as jnp
from jax import lax
from jax.experimental import pallas as pl
from jax.experimental.pallas import tpu as pltpu
from jax.sharding import PartitionSpec as P

TOUCH = 6
BAND = 8
FRONT = 4
BEFORE = BAND - 1
WINDOW = 2 * BAND - 2 + FRONT
PAIRS = TOUCH * (TOUCH + 1) // 2
GROUP = 8
SPAN = 2 * BAND - 1
AXES = ("pts", "grp")
PRECISE = lax.Precision.HIGHEST
VM = pltpu.VMEM
SM = pltpu.SMEM


def spec(space):
    return pl.BlockSpec(memory_space=space)


def call(kernel, out_shapes, args, spaces, scratch=(), flops=0, nbytes=0):
    return pl.pallas_call(
        kernel,
        out_shape=out_shapes,
        in_specs=[spec(s) for s in spaces],
        out_specs=jax.tree.map(lambda _: spec(VM), out_shapes),
        scratch_shapes=list(scratch),
        cost_estimate=pl.CostEstimate(flops=flops, bytes_accessed=nbytes, transcendentals=0),
        compiler_params=pltpu.CompilerParams(vmem_limit_bytes=56 << 20),
    )(*args)


def nt(a, b, precision=None):
    return lax.dot_general(
        a, b, (((1,), (1,)), ((), ())), precision=precision, preferred_element_type=jnp.float32
    )


def tn(a, b, precision=None):
    return lax.dot_general(
        a, b, (((0,), (0,)), ((), ())), precision=precision, preferred_element_type=jnp.float32
    )


def nn(a, b, precision=None):
    return lax.dot_general(
        a, b, (((1,), (0,)), ((), ())), precision=precision, preferred_element_type=jnp.float32
    )


def pair_index(a, b):
    return (TOUCH - 1) * a - (a * (a - 1)) // 2 + b


def pair_kernel(dims, order, slots, jac, blocks, grad, cam, out, scaled, plain, rhs):
    rows, points, piece, grp_count = dims
    v00, v11, v22 = blocks[0:1, :], blocks[1:2, :], blocks[2:3, :]
    v01, v02, v12 = blocks[3:4, :], blocks[4:5, :], blocks[5:6, :]
    a00 = v11 * v22 - v12 * v12
    a11 = v00 * v22 - v02 * v02
    a22 = v00 * v11 - v01 * v01
    a01 = v02 * v12 - v01 * v22
    a02 = v01 * v12 - v11 * v02
    a12 = v01 * v02 - v00 * v12
    inv = 1.0 / (v00 * a00 + v01 * a01 + v02 * a02)
    vinv = [
        [a00 * inv, a01 * inv, a02 * inv],
        [a01 * inv, a11 * inv, a12 * inv],
        [a02 * inv, a12 * inv, a22 * inv],
    ]
    rhs[...] = jnp.zeros_like(rhs)
    rhs[0:1, :] = cam[...]
    for a in range(TOUCH):
        k = order[a]
        parts = [jac[c, k] for c in range(3)]
        wide = [x.astype(jnp.float32) for x in parts]
        for c in range(3):
            total = wide[0] * vinv[0][c] + wide[1] * vinv[1][c] + wide[2] * vinv[2][c]
            scaled[a, :, c * points : (c + 1) * points] = total.astype(jnp.bfloat16)
            plain[a * rows : (a + 1) * rows, c * points : (c + 1) * points] = parts[c]
    for a in range(TOUCH):
        left = scaled[a]
        pulled = nt(grad[...], left)
        t = slots[a]
        rhs[pl.ds(t, 1), :] = rhs[pl.ds(t, 1), :] - pulled[0:1, :]
        tiles = nt(left, plain[a * rows : TOUCH * rows, :])
        for b in range(a, TOUCH):
            at = pair_index(a, b) * piece
            for e in range(GROUP):
                first = (e % grp_count) * (rows // grp_count) + (e // grp_count) * piece
                out[e, at : at + piece, :] = tiles[
                    first : first + piece, (b - a) * rows : (b - a + 1) * rows
                ]
    for e in range(GROUP):
        out[e, PAIRS * piece : PAIRS * piece + BAND, :] = rhs[...]


def merge_kernel(dims, owner, pick, meta, got, out, rhs):
    piece, pts_count, capacity = dims
    base = meta[0]
    for row in range(SPAN):
        for offset in range(BAND):
            if row + offset >= SPAN:
                continue
            total = None
            for j in range(GROUP):
                t = row - j
                if t < 0 or t + offset > BAND - 1:
                    continue
                at = pick[j * BAND * BAND + t * BAND + offset]
                start = pl.multiple_of(jnp.maximum(at, 0) * piece, piece)
                value = jnp.where(at >= 0, got[j, pl.ds(start, piece), :], 0.0)
                total = value if total is None else total + value
            relative = BAND * row + offset
            dest = owner[lax.rem(base + relative, pts_count)]
            slot = relative // pts_count
            out[dest, slot * piece : (slot + 1) * piece, :] = total
    rhs[...] = jnp.zeros_like(rhs)
    for j in range(GROUP):
        rhs[j : j + BAND, :] = rhs[j : j + BAND, :] + got[j, PAIRS * piece : PAIRS * piece + BAND, :]
    for dest in range(pts_count):
        out[dest, capacity * piece : capacity * piece + 2 * BAND, :] = rhs[...]


def owner_kernel(dims, meta, damping, got, rows_out, direct, mirror, reduced):
    piece, pts_count, capacity, grp_count, quarter, clusters, sets, peers = dims
    residue, my_grp, start = meta[0], meta[1], meta[2]
    halves = GROUP // grp_count
    planes = clusters // GROUP
    cols = rows_out.shape[2]
    offset = lax.rem(residue, BAND)
    part = residue // BAND
    stride = pts_count // BAND
    diag = (
        lax.broadcasted_iota(jnp.int32, (quarter, cols), 0) + my_grp * quarter
        == lax.broadcasted_iota(jnp.int32, (quarter, cols), 1)
    )
    diag = diag & (offset == 0)
    for m in range(BAND * grp_count):
        home = (residue + pts_count * m) // BAND
        plane = home // GROUP
        row = lax.rem(home, GROUP)
        before = lax.rem(plane + planes - 1, planes)
        near = (BAND * row + offset) // pts_count
        far = (BAND * (row + GROUP) + offset) // pts_count
        has_far = row + GROUP + offset < SPAN
        far = jnp.where(has_far, far, 0)
        for y in range(halves):
            value = got[plane * halves + y, pl.ds(pl.multiple_of(near * piece, piece), piece), :]
            extra = got[before * halves + y, pl.ds(pl.multiple_of(far * piece, piece), piece), :]
            rows_out[m, y * piece : (y + 1) * piece, :] = value + jnp.where(has_far, extra, 0.0)
        rows_out[m] = rows_out[m] + jnp.where(diag, damping[pl.ds(home, 1), :], 0.0)
    for i in range(sets):
        j = lax.rem(part + 2 * clusters - start, stride) + stride * i
        home = lax.rem(start + jnp.minimum(j, FRONT - 1), clusters)
        value = rows_out[(BAND * home + offset) // pts_count]
        j = lax.rem(part + 2 * clusters - start + offset, stride) + stride * i
        home = lax.rem(start + jnp.minimum(j, FRONT - 1) + clusters - offset, clusters)
        other = rows_out[(BAND * home + offset) // pts_count]
        for peer in range(peers):
            direct[peer, i * quarter : (i + 1) * quarter, :] = value
            mirror[peer, i * quarter : (i + 1) * quarter, :] = other
    tail = capacity * piece
    for plane in range(planes):
        before = (plane + planes - 1) % planes
        reduced[plane * GROUP : (plane + 1) * GROUP, :] = (
            got[plane * halves, tail : tail + BAND, :]
            + got[before * halves, tail + BAND : tail + 2 * BAND, :]
        )


def fetch(own, other, parity, owner, tile, slot, dims):
    pts_count, grp_count, quarter = dims
    source = owner[lax.rem(tile, pts_count)]
    parts = []
    for g in range(grp_count):
        at = (source * grp_count + g) // 2
        mine = own[at, slot * quarter : (slot + 1) * quarter, :]
        theirs = other[at, slot * quarter : (slot + 1) * quarter, :]
        parts.append(jnp.where(parity == g % 2, mine, theirs))
    return jnp.concatenate(parts, axis=0)


def factor_kernel(dims, meta, owner, own, other, reduced, upper, inverse, behind, work, square):
    pts_count, grp_count, quarter, clusters = dims
    rows = work.shape[0]
    parity, start = meta[3], meta[2]
    stride = pts_count // BAND
    after = BAND - 1
    last = after * rows
    behind[...] = jnp.zeros_like(behind)
    upper[...] = jnp.zeros_like(upper)
    for j in range(FRONT):
        home = lax.rem(start + j, clusters)
        for e in range(BAND):
            tile = fetch(
                own, other, parity, owner, BAND * home + e, j // stride,
                (pts_count, grp_count, quarter),
            )
            if j + e < FRONT:
                if e == 0:
                    tile = 0.5 * (tile + tile.T)
                square[j, :, (j + e) * rows : (j + e + 1) * rows] = tile
            else:
                at = (j + e - FRONT) * rows
                behind[at : at + rows, j * rows : (j + 1) * rows] = tile.T
        behind[last : last + 1, j * rows : (j + 1) * rows] = reduced[pl.ds(home, 1), :]
    row_id = lax.broadcasted_iota(jnp.int32, (rows, 1), 0)
    col_id = lax.broadcasted_iota(jnp.int32, (1, rows), 1)
    eye = (row_id == col_id).astype(jnp.float32)
    for j in range(FRONT):
        work[:, 0:rows] = square[j, :, j * rows : (j + 1) * rows]
        work[:, rows : 2 * rows] = eye

        def step(k, carry):
            left = work[:, 0:rows]
            column = jnp.sum(jnp.where(col_id == k, left, 0.0), axis=1, keepdims=True)
            line = work[pl.ds(k, 1), :]
            pivot = jnp.sum(jnp.where(col_id == k, line[:, 0:rows], 0.0), axis=1, keepdims=True)
            scale = jnp.where(row_id > k, column * (1.0 / pivot), 0.0)
            work[...] = work[...] - scale * line
            return carry

        lax.fori_loop(0, rows, step, 0)
        left = work[:, 0:rows]
        pivots = jnp.sum(jnp.where(row_id == col_id, left, 0.0), axis=1, keepdims=True)
        norm = lax.rsqrt(pivots)
        solve = jnp.where(row_id >= col_id, work[:, rows : 2 * rows], 0.0) * norm
        inverse[j] = solve
        upper[j, :, j * rows : (j + 1) * rows] = jnp.where(row_id <= col_id, left, 0.0) * norm
        if j < FRONT - 1:
            upper[j, :, (j + 1) * rows :] = nn(solve, square[j, :, (j + 1) * rows :], PRECISE)
        for i in range(j + 1, FRONT):
            square[i, :, i * rows :] = square[i, :, i * rows :] - tn(
                upper[j, :, i * rows : (i + 1) * rows], upper[j, :, i * rows :], PRECISE
            )
    substitute(behind, upper, inverse, rows)


def substitute(panel, upper, inverse, rows):
    for j in range(FRONT):
        block = panel[:, j * rows : (j + 1) * rows]
        for k in range(j):
            block = block - nn(
                panel[:, k * rows : (k + 1) * rows],
                upper[k, :, j * rows : (j + 1) * rows],
                PRECISE,
            )
        panel[:, j * rows : (j + 1) * rows] = nt(block, inverse[j], PRECISE)


def update_kernel(
    dims, meta, owner, own, other, reduced, upper, inverse, behind, owned,
    tiles_out, rhs_out, panel_out, ahead, panel,
):
    pts_count, grp_count, quarter, clusters = dims
    rows = tiles_out.shape[1]
    width = FRONT * rows
    residue, my_grp, start, parity, device = meta[0], meta[1], meta[2], meta[3], meta[4]
    stride = pts_count // BAND
    ahead[...] = jnp.zeros_like(ahead)
    for j in range(FRONT):
        for i in range(j, BEFORE):
            e = BEFORE + j - i
            if e > BEFORE:
                continue
            home = lax.rem(start + j + clusters - e, clusters)
            tile = fetch(
                own, other, parity, owner, BAND * home + e, j // stride,
                (pts_count, grp_count, quarter),
            )
            ahead[i * rows : (i + 1) * rows, j * rows : (j + 1) * rows] = tile
    substitute(ahead, upper, inverse, rows)
    first = pl.ds(pl.multiple_of(my_grp * rows, rows), rows)
    for i in range(BEFORE):
        panel[i] = ahead[i * rows : (i + 1) * rows, :]
        panel[BEFORE + FRONT + i] = behind[i * rows : (i + 1) * rows, :]
    panel_out[0 : BEFORE * rows, :] = ahead[:, first]
    for j in range(FRONT):
        at = (BEFORE + j) * rows
        panel_out[at : at + rows, :] = upper[my_grp, :, j * rows : (j + 1) * rows].T
    panel_out[(BEFORE + FRONT) * rows :, :] = behind[0 : BEFORE * rows, first]
    base = start + clusters - BEFORE

    def rest(position):
        return (position < WINDOW) & ((position < BEFORE) | (position >= BEFORE + FRONT))

    for i in range(BAND):
        tile = residue + pts_count * (BAND * my_grp + i)
        home = tile // BAND
        offset = lax.rem(tile, BAND)
        one = lax.rem(home + 2 * clusters - base, clusters)
        two = lax.rem(home + offset + 2 * clusters - base, clusters)
        for g in range(grp_count):
            tiles_out[i, g * quarter : (g + 1) * quarter, :] = owned[g, i]

        @pl.when(rest(one) & rest(two))
        def _():
            tiles_out[i] = tiles_out[i] - nt(panel[one], panel[two], PRECISE)

    position = lax.rem(device + 2 * clusters - base, clusters)
    mine = reduced[pl.ds(device, 1), :]
    rhs_out[...] = mine
    last = BEFORE * rows

    @pl.when(rest(position))
    def _():
        moved = nt(behind[last : last + 8, :], panel[position], PRECISE)
        rhs_out[...] = mine - moved[0:1, :]

    @pl.when((position >= BEFORE) & (position < BEFORE + FRONT))
    def _():
        at = pl.multiple_of((position - BEFORE) * rows, rows)
        rhs_out[...] = behind[last : last + 1, pl.ds(at, rows)]


def per_device(
    jacobian, point_blocks, point_grad, camera_grad, damping, incidence, tile_owner, front_first
):
    pts_count = lax.axis_size("pts")
    grp_count = lax.axis_size("grp")
    clusters = pts_count * grp_count
    my_grp = lax.axis_index("grp")
    my_pts = lax.axis_index("pts")
    device = my_pts * grp_count + my_grp
    rows = jacobian.shape[2]
    points = jacobian.shape[4]
    piece = rows // GROUP
    quarter = rows // grp_count
    capacity = (BAND * (SPAN - 1)) // pts_count + 1
    stride = pts_count // BAND
    sets = -(-FRONT // stride)
    peers = clusters // 2
    f32 = jnp.float32
    groups = [[GROUP * z + e for e in range(GROUP)] for z in range(clusters // GROUP)]
    same = [[2 * i + c for i in range(peers)] for c in range(2)]
    swap = [(i, i ^ 1) for i in range(clusters)]

    def exchange(value, lists):
        return lax.all_to_all(
            value, AXES, split_axis=0, concat_axis=0, tiled=True, axis_index_groups=lists
        )

    slot = jnp.mod(incidence[0] - device, clusters)
    spread = jnp.broadcast_to(jnp.pad(slot, (0, 2))[None, :], (GROUP, BAND))
    member_slots = exchange(spread, groups)[:, :TOUCH]
    rank = jnp.sum(slot[None, :] < slot[:, None], axis=1)
    placed = rank[None, :] == jnp.arange(TOUCH)[:, None]
    order = jnp.sum(jnp.where(placed, jnp.arange(TOUCH)[None, :], 0), axis=1).astype(jnp.int32)
    sorted_slots = jnp.sum(jnp.where(placed, slot[None, :], 0), axis=1).astype(jnp.int32)
    jac = jnp.transpose(jacobian[0], (2, 0, 1, 3))
    grad = jnp.broadcast_to(point_grad.reshape(1, 3 * points), (16, 3 * points))
    block_rows = PAIRS * piece + BAND
    sent = call(
        functools.partial(pair_kernel, (rows, points, piece, grp_count)),
        jax.ShapeDtypeStruct((GROUP, block_rows, rows), f32),
        (order, sorted_slots, jac, point_blocks[0], grad, camera_grad),
        (SM, SM, VM, VM, VM, VM),
        (
            pltpu.VMEM((TOUCH, rows, 3 * points), jnp.bfloat16),
            pltpu.VMEM((TOUCH * rows, 3 * points), jnp.bfloat16),
            pltpu.VMEM((BAND, rows), f32),
        ),
        flops=2 * PAIRS * rows * rows * 3 * points,
        nbytes=4 * GROUP * block_rows * rows,
    )
    got = exchange(sent, groups)

    here = member_slots[:, None, :] == jnp.arange(BAND)[None, :, None]
    present = jnp.any(here, axis=2)
    less = jnp.sum(
        (member_slots[:, None, :] < jnp.arange(BAND)[None, :, None]).astype(jnp.int32), axis=2
    )
    later = jnp.arange(BAND)[:, None] + jnp.arange(BAND)[None, :]
    at_later = later[:, :, None] == jnp.arange(BAND)[None, None, :]
    less_later = jnp.sum(jnp.where(at_later[None], less[:, None, None, :], 0), axis=3)
    present_later = jnp.any(at_later[None] & present[:, None, None, :], axis=3)
    pick = jnp.where(
        present[:, :, None] & present_later, pair_index(less[:, :, None], less_later), -1
    )
    pick = pick.reshape(GROUP * BAND * BAND).astype(jnp.int32)
    residue = jnp.sum(jnp.arange(pts_count) * (tile_owner == my_pts))
    group_base = jnp.mod((device // GROUP) * GROUP * BAND, pts_count)
    send_rows = capacity * piece + 2 * BAND
    sent = call(
        functools.partial(merge_kernel, (piece, pts_count, capacity)),
        jax.ShapeDtypeStruct((pts_count, send_rows, rows), f32),
        (tile_owner, pick, group_base[None].astype(jnp.int32), got),
        (SM, SM, SM, VM),
        (pltpu.VMEM((2 * BAND, rows), f32),),
        nbytes=4 * (pts_count * send_rows + GROUP * block_rows) * rows,
    )
    got = lax.all_to_all(sent, "pts", split_axis=0, concat_axis=0, tiled=True)

    lane = jnp.arange(8)
    meta = jnp.where(lane == 0, residue, 0)
    meta = jnp.where(lane == 1, my_grp, meta)
    meta = jnp.where(lane == 2, front_first[0], meta)
    meta = jnp.where(lane == 3, jnp.mod(device, 2), meta)
    meta = jnp.where(lane == 4, device, meta).astype(jnp.int32)
    owner_rows, direct, mirror, reduced = call(
        functools.partial(
            owner_kernel,
            (piece, pts_count, capacity, grp_count, quarter, clusters, sets, peers),
        ),
        (
            jax.ShapeDtypeStruct((BAND * grp_count, quarter, rows), f32),
            jax.ShapeDtypeStruct((peers, sets * quarter, rows), f32),
            jax.ShapeDtypeStruct((peers, sets * quarter, rows), f32),
            jax.ShapeDtypeStruct((clusters, rows), f32),
        ),
        (meta, damping, got),
        (SM, VM, VM),
        nbytes=4 * (pts_count * send_rows + 2 * peers * sets * quarter) * rows,
    )
    direct = exchange(direct, same)
    direct_other = lax.ppermute(direct, AXES, swap)
    mirror = exchange(mirror, same)
    mirror_other = lax.ppermute(mirror, AXES, swap)
    owned = lax.all_to_all(owner_rows, "grp", split_axis=0, concat_axis=0, tiled=True)
    owned = owned.reshape(grp_count, BAND, quarter, rows)

    width = FRONT * rows
    dims = (pts_count, grp_count, quarter, clusters)
    upper, inverse, behind = call(
        functools.partial(factor_kernel, dims),
        (
            jax.ShapeDtypeStruct((FRONT, rows, width), f32),
            jax.ShapeDtypeStruct((FRONT, rows, rows), f32),
            jax.ShapeDtypeStruct((BEFORE * rows + 8, width), f32),
        ),
        (meta, tile_owner, direct, direct_other, reduced),
        (SM, SM, VM, VM, VM),
        (
            pltpu.VMEM((rows, 2 * rows), f32),
            pltpu.VMEM((FRONT, rows, width), f32),
        ),
        flops=400 * rows * rows * rows * 6,
        nbytes=8 * peers * sets * quarter * rows,
    )
    tiles_out, rhs_out, front_panel = call(
        functools.partial(update_kernel, dims),
        (
            jax.ShapeDtypeStruct((BAND, rows, rows), f32),
            jax.ShapeDtypeStruct((1, rows), f32),
            jax.ShapeDtypeStruct((WINDOW * rows, rows), f32),
        ),
        (meta, tile_owner, mirror, mirror_other, reduced, upper, inverse, behind, owned),
        (SM, SM, VM, VM, VM, VM, VM, VM, VM),
        (
            pltpu.VMEM((BEFORE * rows, width), f32),
            pltpu.VMEM((WINDOW, rows, width), f32),
        ),
        flops=200 * rows * rows * rows * 6,
        nbytes=8 * peers * sets * quarter * rows,
    )
    return (tiles_out, rhs_out, front_panel)


def solution(mesh):
    in_specs = (
        P(AXES, None, None, None, None),
        P(AXES, None, None),
        P(AXES, None, None),
        P(AXES, None),
        P(),
        P(AXES, None),
        P(),
        P(),
    )
    out_specs = (P(AXES, None, None), P(AXES, None), P(None, "grp"))
    return jax.shard_map(
        per_device, mesh=mesh, in_specs=in_specs, out_specs=out_specs, check_vma=False
    )
```

```python
import functools

import jax
import jax.numpy as jnp
from jax import lax
from jax.experimental import pallas as pl
from jax.experimental.pallas import tpu as pltpu
from jax.sharding import PartitionSpec as P

TOUCH = 6
BAND = 8
FRONT = 4
BEFORE = BAND - 1
WINDOW = 2 * BAND - 2 + FRONT
PAIRS = TOUCH * (TOUCH + 1) // 2
GROUP = 8
SPAN = 2 * BAND - 1
STRIP = 8
AXES = ("pts", "grp")
VM = pltpu.VMEM
HB = pltpu.HBM
SM = pltpu.SMEM


def spec(space):
    return pl.BlockSpec(memory_space=space)


def size_of(shape, dtype):
    total = jnp.dtype(dtype).itemsize
    for extent in shape:
        total *= extent
    return total


def call(kernel, out_shapes, args, spaces, scratch=(), flops=0, out_spaces=None):
    moved = sum(size_of(x.shape, x.dtype) for x, s in zip(args, spaces) if s is VM)
    moved += sum(size_of(x.shape, x.dtype) for x in jax.tree.leaves(out_shapes))
    kept = 0
    for x in scratch:
        if x.memory_space is VM:
            kept += size_of(x.shape, x.dtype)
    limit = min(moved + kept + (8 << 20), 60 << 20)
    return pl.pallas_call(
        kernel,
        out_shape=out_shapes,
        in_specs=[spec(s) for s in spaces],
        out_specs=[spec(s) for s in out_spaces or [VM] * len(out_shapes)],
        scratch_shapes=list(scratch),
        cost_estimate=pl.CostEstimate(flops=flops, bytes_accessed=moved, transcendentals=0),
        compiler_params=pltpu.CompilerParams(vmem_limit_bytes=limit),
    )(*args)


NT = (((1,), (1,)), ((), ()))
TN = (((0,), (0,)), ((), ()))
NN = (((1,), (0,)), ((), ()))


def product(a, b, dims):
    return lax.dot_general(a, b, dims, preferred_element_type=jnp.float32)


def halves(x):
    high = x.astype(jnp.bfloat16)
    return high, (x - high.astype(jnp.float32)).astype(jnp.bfloat16)


def product3(a, b, dims):
    return (
        product(a[0], b[0], dims) + product(a[0], b[1], dims) + product(a[1], b[0], dims)
    )


def pair_index(a, b):
    return (TOUCH - 1) * a - (a * (a - 1)) // 2 + b


def pair_kernel(dims, meta, incidence, jac, blocks, grad, cam, *refs):
    rows, points, piece, grp_count, clusters = dims
    outs, (out, scaled, plain, rhs, pulls) = refs[:GROUP], refs[GROUP:]
    slots = [lax.rem(incidence[0, k] + clusters - meta[2], clusters) for k in range(TOUCH)]
    ranks = [
        sum((slots[m] < slots[k]).astype(jnp.int32) for m in range(TOUCH) if m != k)
        for k in range(TOUCH)
    ]
    v00, v11, v22 = blocks[0:1, :], blocks[1:2, :], blocks[2:3, :]
    v01, v02, v12 = blocks[3:4, :], blocks[4:5, :], blocks[5:6, :]
    a00 = v11 * v22 - v12 * v12
    a11 = v00 * v22 - v02 * v02
    a22 = v00 * v11 - v01 * v01
    a01 = v02 * v12 - v01 * v22
    a02 = v01 * v12 - v11 * v02
    a12 = v01 * v02 - v00 * v12
    inv = 1.0 / (v00 * a00 + v01 * a01 + v02 * a02)
    vinv = [
        [a00 * inv, a01 * inv, a02 * inv],
        [a01 * inv, a11 * inv, a12 * inv],
        [a02 * inv, a12 * inv, a22 * inv],
    ]
    rhs[...] = jnp.zeros_like(rhs)
    rhs[0:1, :] = cam[...]
    wide_grad = grad[...].astype(jnp.float32)
    for c in range(3):
        pulls[:, c * points : (c + 1) * points] = jnp.broadcast_to(
            wide_grad[c : c + 1, :], (16, points)
        ).astype(jnp.bfloat16)
    for a in range(TOUCH):
        k = sum(jnp.where(ranks[m] == a, m, 0) for m in range(TOUCH))
        t = sum(jnp.where(ranks[m] == a, slots[m], 0) for m in range(TOUCH))
        parts = [jac[c, k] for c in range(3)]
        wide = [x.astype(jnp.float32) for x in parts]
        for c in range(3):
            total = wide[0] * vinv[0][c] + wide[1] * vinv[1][c] + wide[2] * vinv[2][c]
            scaled[a, :, c * points : (c + 1) * points] = total.astype(jnp.bfloat16)
            plain[a * rows : (a + 1) * rows, c * points : (c + 1) * points] = parts[c]
        pulled = product(pulls[...], scaled[a], NT)
        rhs[pl.ds(t, 1), :] = rhs[pl.ds(t, 1), :] - pulled[0:1, :]
    for a in range(TOUCH):
        tiles = product(scaled[a], plain[a * rows : TOUCH * rows, :], NT)
        for b in range(a, TOUCH):
            at = pair_index(a, b) * piece
            for e in range(GROUP):
                first = (e % grp_count) * (rows // grp_count) + (e // grp_count) * piece
                out[e, at : at + piece, :] = tiles[
                    first : first + piece, (b - a) * rows : (b - a + 1) * rows
                ]
    lane = lax.broadcasted_iota(jnp.int32, (BAND, rows), 1)
    early = lax.rem(lane // BAND, BAND)
    late = early + lax.rem(lane, BAND)
    ones = jnp.ones_like(lane)
    none = jnp.zeros_like(lane)
    less, less_late, hit, hit_late = none, none, none, none
    for k in range(TOUCH):
        less = less + jnp.where(early > slots[k], ones, none)
        less_late = less_late + jnp.where(late > slots[k], ones, none)
        hit = hit + jnp.where(early == slots[k], ones, none)
        hit_late = hit_late + jnp.where(late == slots[k], ones, none)
    pick = jnp.where(hit * hit_late > 0, pair_index(less, less_late), -1).astype(jnp.float32)
    tail = PAIRS * piece
    for e in range(GROUP):
        out[e, tail : tail + BAND, :] = rhs[...]
        out[e, tail + BAND : tail + 2 * BAND, :] = pick
    place = lax.rem(meta[2], GROUP)
    for bit in range(GROUP):
        outs[bit][...] = out[place ^ bit]


def merge_kernel(dims, owner, meta, *refs):
    piece, pts_count, capacity, sends = dims
    arrived, outs = refs[:GROUP], refs[GROUP : GROUP + sends]
    got, out, rhs, table, pick, sem = refs[GROUP + sends :]
    place = lax.rem(meta[2], GROUP)
    for bit in range(GROUP):
        got[place ^ bit] = arrived[bit][...]
    flip = meta[0] if sends > 1 else 0
    base = lax.rem(meta[2] // GROUP * (GROUP * BAND), pts_count)
    tail = PAIRS * piece
    for j in range(GROUP):
        row = got[j, tail + BAND : tail + 2 * BAND, :]
        table[j : j + 1, :] = row[0:1, :].astype(jnp.int32)
    copy = pltpu.make_async_copy(table, pick, sem)
    copy.start()
    copy.wait()
    for row in range(SPAN):
        for offset in range(BAND):
            if row + offset >= SPAN:
                continue
            total = None
            for j in range(GROUP):
                t = row - j
                if t < 0 or t + offset > BAND - 1:
                    continue
                at = pick[j, t * BAND + offset]
                start = pl.multiple_of(jnp.maximum(at, 0) * piece, piece)
                value = jnp.where(at >= 0, got[j, pl.ds(start, piece), :], 0.0)
                total = value if total is None else total + value
            relative = BAND * row + offset
            dest = owner[lax.rem(base + relative, pts_count)]
            slot = relative // pts_count
            out[dest ^ flip, slot * piece : (slot + 1) * piece, :] = total
    rhs[...] = jnp.zeros_like(rhs)
    for j in range(GROUP):
        rhs[j : j + BAND, :] = rhs[j : j + BAND, :] + got[j, PAIRS * piece : PAIRS * piece + BAND, :]
    for dest in range(pts_count):
        out[dest, capacity * piece : capacity * piece + 2 * BAND, :] = rhs[...]
    for bit in range(sends):
        outs[bit][...] = out[bit] if sends > 1 else out[...]


def residue_of(owner, meta, pts_count):
    return sum(jnp.where(owner[i] == meta[0], i, 0) for i in range(pts_count))


def owner_kernel(
    dims, owner, meta, front, damping, *refs
):
    piece, pts_count, capacity, grp_count, quarter, clusters, sets, sends = dims
    arrived = refs[:sends]
    outs = refs[sends : sends + grp_count]
    direct, mirror, reduced, got, rows_out = refs[sends + grp_count :]
    for bit in range(sends):
        if sends > 1:
            got[meta[0] ^ bit] = arrived[bit][...]
        else:
            got[...] = arrived[0][...]
    residue, my_grp, start = residue_of(owner, meta, pts_count), meta[1], front[0]
    members = GROUP // grp_count
    planes = clusters // GROUP
    cols = rows_out.shape[3]
    offset = lax.rem(residue, BAND)
    part = residue // BAND
    stride = pts_count // BAND
    diag = (
        lax.broadcasted_iota(jnp.int32, (quarter, cols), 0) + my_grp * quarter
        == lax.broadcasted_iota(jnp.int32, (quarter, cols), 1)
    )
    diag = diag & (offset == 0)
    for m in range(BAND * grp_count):
        home = (residue + pts_count * m) // BAND
        plane = home // GROUP
        row = lax.rem(home, GROUP)
        before = lax.rem(plane + planes - 1, planes)
        near = (BAND * row + offset) // pts_count
        far = (BAND * (row + GROUP) + offset) // pts_count
        has_far = row + GROUP + offset < SPAN
        far = jnp.where(has_far, far, 0)
        for y in range(members):
            value = got[plane * members + y, pl.ds(pl.multiple_of(near * piece, piece), piece), :]
            extra = got[before * members + y, pl.ds(pl.multiple_of(far * piece, piece), piece), :]
            total = value + jnp.where(has_far, extra, 0.0)
            part_diag = diag[y * piece : (y + 1) * piece, :]
            total = total + jnp.where(part_diag, damping[pl.ds(home, 1), :], 0.0)
            rows_out[(m // BAND) ^ my_grp, m % BAND, y * piece : (y + 1) * piece, :] = total
    for i in range(sets):
        j = lax.rem(part + 2 * clusters - start, stride) + stride * i
        home = lax.rem(start + jnp.minimum(j, FRONT - 1), clusters)
        at = (BAND * home + offset) // pts_count
        value = rows_out[(at // BAND) ^ my_grp, lax.rem(at, BAND)]
        j = lax.rem(part + 2 * clusters - start + offset, stride) + stride * i
        home = lax.rem(start + jnp.minimum(j, FRONT - 1) + clusters - offset, clusters)
        at = (BAND * home + offset) // pts_count
        other = rows_out[(at // BAND) ^ my_grp, lax.rem(at, BAND)]
        for layer in range(direct.shape[0]):
            direct[layer, i * quarter : (i + 1) * quarter, :] = value
            mirror[layer, i * quarter : (i + 1) * quarter, :] = other
    for bit in range(grp_count):
        outs[bit][...] = rows_out[bit]
    tail = capacity * piece
    for plane in range(planes):
        before = (plane + planes - 1) % planes
        reduced[plane * GROUP : (plane + 1) * GROUP, :] = (
            got[plane * members, tail : tail + BAND, :]
            + got[before * members, tail + BAND : tail + 2 * BAND, :]
        )


def gather(gathered, sides, meta, clusters, ring):
    layers = clusters // GROUP
    place, level = lax.rem(meta[2], GROUP), meta[2] // GROUP
    for i in range(GROUP // 2):
        for z in range(layers):
            at = lax.rem(level + layers - z, layers) if ring else z
            at = at * GROUP + (place ^ (2 * i))
            gathered[at] = sides[i][z]
            gathered[at ^ 1] = sides[GROUP // 2 + i][z]


def fetch(gathered, owner, tile, slot, dims):
    pts_count, grp_count, quarter = dims
    source = owner[lax.rem(tile, pts_count)] * grp_count
    rows = slice(slot * quarter, (slot + 1) * quarter)
    return jnp.concatenate([gathered[source + g, rows, :] for g in range(grp_count)], axis=0)


def factor_kernel(dims, meta, front, owner, reduced, *refs):
    pts_count, grp_count, quarter, clusters, ring = dims
    sides = refs[:GROUP]
    outs, refs = refs[GROUP : GROUP + 5], refs[GROUP + 5 :]
    tail_out, solve_high, solve_low, behind_high, behind_low = refs[:5]
    upper, behind, gathered, work, done, square, wide, sems = refs[5:]
    rows = done.shape[0]
    width = FRONT * rows
    start = front[0]
    stride = pts_count // BAND
    after = BAND - 1
    last = after * rows
    gather(gathered, sides, meta, clusters, ring)
    work[rows:, :] = jnp.zeros((STRIP, 2 * rows), jnp.float32)
    wide[...] = jnp.zeros_like(wide)
    upper[...] = jnp.zeros_like(upper)
    square[...] = jnp.zeros_like(square)
    row_id = lax.broadcasted_iota(jnp.int32, (rows, 1), 0)
    col_id = lax.broadcasted_iota(jnp.int32, (1, rows), 1)
    eye = (row_id == col_id).astype(jnp.float32)
    for j in range(FRONT):
        home = lax.rem(start + j, clusters)
        for e in range(BAND):
            tile = fetch(
                gathered, owner, BAND * home + e, j // stride, (pts_count, grp_count, quarter)
            )
            if j + e < FRONT:
                if e == 0:
                    tile = 0.5 * (tile + tile.T)
                square[j, :, (j + e) * rows : (j + e + 1) * rows] = tile
            else:
                at = (j + e - FRONT) * rows
                wide[at : at + rows, j * rows : (j + 1) * rows] = tile.T
        wide[last : last + 1, j * rows : (j + 1) * rows] = reduced[pl.ds(home, 1), :]
    for j in range(FRONT):
        here = j * rows
        work[0:rows, 0:rows] = square[j, :, here : here + rows]
        work[0:rows, rows : 2 * rows] = eye
        eliminate(work, done, rows)
        inverse = jnp.where(row_id >= col_id, done[:, rows : 2 * rows], 0.0)
        pair = halves(inverse)
        upper[j, :, here : here + rows] = jnp.where(row_id <= col_id, done[:, 0:rows], 0.0)
        parts = []
        if j < FRONT - 1:
            parts.append(square[j, :, here + rows : width])
        if j > 0:
            parts.append(square[j, :, width : width + here])
        line = product3(pair, halves(jnp.concatenate(parts, axis=1)), NN)
        ahead = width - here - rows
        if ahead:
            upper[j, :, here + rows :] = line[:, 0:ahead]
        solve = jnp.concatenate([line[:, ahead:], inverse], axis=1) if j else inverse
        high, low = halves(solve)
        solve_high[here : here + rows, 0 : here + rows] = high
        solve_low[here : here + rows, 0 : here + rows] = low
        if j < FRONT - 1:
            zero = jnp.zeros((rows, ahead), jnp.bfloat16)
            solve_high[here : here + rows, here + rows :] = zero
            solve_low[here : here + rows, here + rows :] = zero
            both = halves(line[:, 0:ahead])
            for i in range(j + 1, FRONT):
                skip = (i - j - 1) * rows
                left = tuple(x[:, skip : skip + rows] for x in both)
                right = tuple(
                    jnp.concatenate([x[:, skip:], y], axis=1) for x, y in zip(both, (high, low))
                )
                change = product3(left, right, TN)
                cut = width - i * rows
                square[i, :, i * rows : width] = square[i, :, i * rows : width] - change[:, 0:cut]
                square[i, :, width : width + here + rows] = (
                    square[i, :, width : width + here + rows] - change[:, cut:]
                )
    result = product3(halves(wide[...]), (solve_high[...], solve_low[...]), NT)
    high, low = halves(result)
    behind_high[...] = high
    behind_low[...] = low
    behind[...] = result
    first = pl.ds(pl.multiple_of(meta[1] * rows, rows), rows)
    for j in range(FRONT):
        tail_out[j * rows : (j + 1) * rows, :] = upper[meta[1], :, j * rows : (j + 1) * rows].T
    tail_out[FRONT * rows : FRONT * rows + last, :] = behind[0:last, first]
    for j in range(FRONT):
        at = FRONT * rows + last + 8 * j
        tail_out[at : at + 8, :] = result[last : last + 8, j * rows : (j + 1) * rows]
    copies = [
        pltpu.make_async_copy(source, target, sems.at[i])
        for i, (source, target) in enumerate(zip(refs[:5], outs))
    ]
    for copy in copies:
        copy.start()
    for copy in copies:
        copy.wait()


def eliminate(work, done, rows):
    lanes = lax.broadcasted_iota(jnp.int32, (STRIP, rows), 1)
    subs = lax.broadcasted_iota(jnp.int32, (STRIP, rows), 0)

    def strip(p, carry):
        now, past = carry
        at = pl.multiple_of(p * STRIP, STRIP)
        lhs = jnp.where(lanes >= at + STRIP, past[:, 0:rows], 0.0)
        work[0:rows, :] = work[0:rows, :] - product3(halves(lhs), halves(past), TN)
        ahead = work[pl.ds(at + STRIP, STRIP), :]
        now_a, now_i = now[:, 0:rows], now[:, rows : 2 * rows]
        next_a, next_i = ahead[:, 0:rows], ahead[:, rows : 2 * rows]
        shift = lax.rem(rows - at, rows)
        turned = pltpu.roll(now_a, shift, 1)
        turned_next = pltpu.roll(next_a, shift, 1)
        column = [jnp.broadcast_to(turned[:, i : i + 1], (STRIP, rows)) for i in range(STRIP)]
        below = [jnp.broadcast_to(turned_next[:, i : i + 1], (STRIP, rows)) for i in range(STRIP)]
        norm = jnp.zeros((STRIP, rows), jnp.float32)
        for i in range(STRIP):
            pivot = jnp.broadcast_to(column[i][i : i + 1, :], (STRIP, rows))
            inv = 1.0 / pivot
            norm = jnp.where(subs == i, lax.rsqrt(pivot), norm)
            scale = jnp.where(subs > i, column[i] * inv, 0.0)
            scale_next = below[i] * inv
            for k in range(i + 1, STRIP):
                top = jnp.broadcast_to(column[k][i : i + 1, :], (STRIP, rows))
                column[k] = column[k] - scale * top
                below[k] = below[k] - scale_next * top
            line_a = jnp.broadcast_to(now_a[i : i + 1, :], (STRIP, rows))
            line_i = jnp.broadcast_to(now_i[i : i + 1, :], (STRIP, rows))
            now_a = now_a - scale * line_a
            now_i = now_i - scale * line_i
            next_a = next_a - scale_next * line_a
            next_i = next_i - scale_next * line_i
        finished = jnp.concatenate([now_a * norm, now_i * norm], axis=1)
        done[pl.ds(at, STRIP), :] = finished
        return (jnp.concatenate([next_a, next_i], axis=1), finished)

    first = work[0:STRIP, :]
    lax.fori_loop(0, rows // STRIP, strip, (first, jnp.zeros_like(first)))


def update_kernel(dims, meta, front, owner, reduced, *refs):
    pts_count, grp_count, quarter, clusters, ring = dims
    sides, refs = refs[:GROUP], refs[GROUP:]
    stored, chunks = refs[:5], refs[5 : 5 + grp_count]
    tiles_out, rhs_out, panel_out, wide, ahead_high, ahead_low, gathered = refs[
        5 + grp_count : 12 + grp_count
    ]
    kept = refs[12 + grp_count : 17 + grp_count]
    tail, solve_high, solve_low, behind_high, behind_low = kept
    sems = refs[17 + grp_count]
    copies = [
        pltpu.make_async_copy(source, target, sems.at[i])
        for i, (source, target) in enumerate(zip(stored, kept))
    ]
    for copy in copies:
        copy.start()
    rows = tiles_out.shape[1]
    residue, my_grp, start = residue_of(owner, meta, pts_count), meta[1], front[0]
    device = meta[2]
    stride = pts_count // BAND
    gather(gathered, sides, meta, clusters, ring)
    wide[...] = jnp.zeros_like(wide)
    for j in range(FRONT):
        for i in range(j, BEFORE):
            e = BEFORE + j - i
            home = lax.rem(start + j + clusters - e, clusters)
            tile = fetch(
                gathered, owner, BAND * home + e, j // stride, (pts_count, grp_count, quarter)
            )
            wide[i * rows : (i + 1) * rows, j * rows : (j + 1) * rows] = tile
    for copy in copies:
        copy.wait()
    result = product3(halves(wide[...]), (solve_high[...], solve_low[...]), NT)
    wide[...] = result
    high, low = halves(result)
    ahead_high[...] = high
    ahead_low[...] = low
    first = pl.ds(pl.multiple_of(my_grp * rows, rows), rows)
    panel_out[0 : BEFORE * rows, :] = wide[:, first]
    panel_out[BEFORE * rows :, :] = tail[0 : (BEFORE + FRONT) * rows, :]
    base = start + clusters - BEFORE

    def ahead(position):
        at = pl.ds(pl.multiple_of(position * rows, rows), rows)
        return (ahead_high[at, :], ahead_low[at, :])

    def past(position):
        at = pl.ds(pl.multiple_of((position - BEFORE - FRONT) * rows, rows), rows)
        return (behind_high[at, :], behind_low[at, :])

    def is_ahead(position):
        return position < BEFORE

    def is_past(position):
        return (position < WINDOW) & (position >= BEFORE + FRONT)

    for i in range(BAND):
        tile = residue + pts_count * (BAND * my_grp + i)
        home = tile // BAND
        offset = lax.rem(tile, BAND)
        one = lax.rem(home + 2 * clusters - base, clusters)
        two = lax.rem(home + offset + 2 * clusters - base, clusters)
        for bit in range(grp_count):
            at = pl.multiple_of((my_grp ^ bit) * quarter, quarter)
            tiles_out[i, pl.ds(at, quarter), :] = chunks[bit][i]
        for left, right, test_left, test_right in (
            (ahead, ahead, is_ahead, is_ahead),
            (ahead, past, is_ahead, is_past),
            (past, past, is_past, is_past),
        ):
            @pl.when(test_left(one) & test_right(two))
            def _():
                tiles_out[i] = tiles_out[i] - product3(left(one), right(two), NT)

    position = lax.rem(device + 2 * clusters - base, clusters)
    mine = reduced[pl.ds(device, 1), :]
    rhs_out[...] = mine
    last = (BEFORE + FRONT) * rows
    front_row = [tail[last + 8 * j : last + 8 * j + 8, :] for j in range(FRONT)]
    for take, test in ((ahead, is_ahead), (past, is_past)):
        @pl.when(test(position))
        def _():
            known = halves(jnp.concatenate(front_row, axis=1))
            rhs_out[...] = mine - product3(known, take(position), NT)[0:1, :]

    @pl.when((position >= BEFORE) & (position < BEFORE + FRONT))
    def _():
        at = pl.multiple_of(last + 8 * (position - BEFORE), 8)
        rhs_out[...] = tail[pl.ds(at, 8), :][0:1, :]


def per_device(
    jacobian, point_blocks, point_grad, camera_grad, damping, incidence, tile_owner, front_first
):
    pts_count = lax.axis_size("pts")
    grp_count = lax.axis_size("grp")
    clusters = pts_count * grp_count
    my_grp = lax.axis_index("grp")
    my_pts = lax.axis_index("pts")
    device = my_pts * grp_count + my_grp
    rows = jacobian.shape[2]
    points = jacobian.shape[4]
    piece = rows // GROUP
    quarter = rows // grp_count
    capacity = (BAND * (SPAN - 1)) // pts_count + 1
    stride = pts_count // BAND
    sets = -(-FRONT // stride)
    f32 = jnp.float32
    layers = clusters // GROUP
    columns = [[GROUP * z + e for z in range(layers)] for e in range(GROUP)]
    swap = [(i, i ^ 1) for i in range(clusters)]

    def flip(values, axis, count):
        moved = [
            lax.ppermute(value, axis, [(p, p ^ (bit + 1)) for p in range(count)])
            for bit, value in enumerate(values[1:])
        ]
        return [values[0], *moved]

    def exchange(value, lists):
        return lax.all_to_all(
            value, AXES, split_axis=0, concat_axis=0, tiled=True, axis_index_groups=lists
        )

    lane = jnp.arange(8)
    meta = jnp.where(lane == 0, my_pts, jnp.where(lane == 1, my_grp, device)).astype(jnp.int32)
    bf16 = jnp.bfloat16
    jac = jnp.transpose(jacobian[0], (2, 0, 1, 3))
    block_rows = PAIRS * piece + 2 * BAND
    sent = call(
        functools.partial(pair_kernel, (rows, points, piece, grp_count, clusters)),
        [jax.ShapeDtypeStruct((block_rows, rows), f32)] * GROUP,
        (meta, incidence, jac, point_blocks[0], point_grad[0], camera_grad),
        (SM, SM, VM, VM, VM, VM),
        (
            pltpu.VMEM((GROUP, block_rows, rows), f32),
            pltpu.VMEM((TOUCH, rows, 3 * points), bf16),
            pltpu.VMEM((TOUCH * rows, 3 * points), bf16),
            pltpu.VMEM((BAND, rows), f32),
            pltpu.VMEM((16, 3 * points), bf16),
        ),
        flops=2 * PAIRS * rows * rows * 3 * points,
    )
    got = flip(sent, AXES, clusters)
    sends = pts_count if pts_count <= GROUP else 1
    send_rows = capacity * piece + 2 * BAND
    shape = (send_rows, rows) if sends > 1 else (pts_count, send_rows, rows)
    sent = call(
        functools.partial(merge_kernel, (piece, pts_count, capacity, sends)),
        [jax.ShapeDtypeStruct(shape, f32)] * sends,
        (tile_owner, meta, *got),
        (SM, SM) + (VM,) * GROUP,
        (
            pltpu.VMEM((GROUP, block_rows, rows), f32),
            pltpu.VMEM((pts_count, send_rows, rows), f32),
            pltpu.VMEM((2 * BAND, rows), f32),
            pltpu.VMEM((GROUP, rows), jnp.int32),
            pltpu.SMEM((GROUP, rows), jnp.int32),
            pltpu.SemaphoreType.DMA(()),
        ),
    )
    if sends > 1:
        got = flip(sent, "pts", pts_count)
    else:
        got = [lax.all_to_all(sent[0], "pts", split_axis=0, concat_axis=0, tiled=True)]
    *chunks, direct, mirror, reduced = call(
        functools.partial(
            owner_kernel,
            (piece, pts_count, capacity, grp_count, quarter, clusters, sets, sends),
        ),
        [jax.ShapeDtypeStruct((BAND, quarter, rows), f32)] * grp_count
        + [
            jax.ShapeDtypeStruct((layers if layers > 4 else 1, sets * quarter, rows), f32),
            jax.ShapeDtypeStruct((layers if layers > 4 else 1, sets * quarter, rows), f32),
            jax.ShapeDtypeStruct((clusters, rows), f32),
        ],
        (tile_owner, meta, front_first, damping, *got),
        (SM, SM, SM, VM) + (VM,) * sends,
        (
            pltpu.VMEM((pts_count, send_rows, rows), f32),
            pltpu.VMEM((grp_count, BAND, quarter, rows), f32),
        ),
    )
    chunks = flip(chunks, "grp", grp_count)
    ring = layers <= 4

    def along(value):
        if not ring:
            return exchange(value, columns)
        moved = [
            lax.ppermute(value, AXES, [(p, (p + GROUP * z) % clusters) for p in range(clusters)])
            for z in range(1, layers)
        ]
        return jnp.concatenate([value, *moved])

    def across(value):
        return [value] + [
            lax.ppermute(value, AXES, [(p, p ^ (2 * i)) for p in range(clusters)])
            for i in range(1, GROUP // 2)
        ]

    direct = along(direct)
    direct, mirror, *chunks = lax.optimization_barrier((direct, mirror, *chunks))
    mirror = along(mirror)
    mirror_other = lax.ppermute(mirror, AXES, swap)
    mine = across(direct)
    mirror, mirror_other, *mine = lax.optimization_barrier((mirror, mirror_other, *mine))
    theirs = [lax.ppermute(x, AXES, swap) for x in mine]
    sides = across(mirror) + across(mirror_other)

    width = FRONT * rows
    dims = (pts_count, grp_count, quarter, clusters)
    tall = BEFORE * rows + 8
    tail = (FRONT + BEFORE) * rows + 8 * FRONT
    shapes = (
        ((tail, rows), f32),
        ((width, width), bf16),
        ((width, width), bf16),
        ((tall, width), bf16),
        ((tall, width), bf16),
    )
    stored = call(
        functools.partial(factor_kernel, dims + (ring,)),
        [jax.ShapeDtypeStruct(*x) for x in shapes],
        (meta, front_first, tile_owner, reduced, *mine, *theirs),
        (SM, SM, SM, VM) + (VM,) * GROUP,
        [pltpu.VMEM(*x) for x in shapes]
        + [
            pltpu.VMEM((FRONT, rows, width), f32),
            pltpu.VMEM((tall, width), f32),
            pltpu.VMEM((clusters, sets * quarter, rows), f32),
            pltpu.VMEM((rows + STRIP, 2 * rows), f32),
            pltpu.VMEM((rows, 2 * rows), f32),
            pltpu.VMEM((FRONT, rows, 2 * width), f32),
            pltpu.VMEM((tall, width), f32),
            pltpu.SemaphoreType.DMA((5,)),
        ],
        flops=400 * rows * rows * rows * 6,
        out_spaces=[HB] * 5,
    )
    return tuple(call(
        functools.partial(update_kernel, dims + (ring,)),
        [
            jax.ShapeDtypeStruct((BAND, rows, rows), f32),
            jax.ShapeDtypeStruct((1, rows), f32),
            jax.ShapeDtypeStruct((WINDOW * rows, rows), f32),
        ],
        (meta, front_first, tile_owner, reduced, *sides, *stored, *chunks),
        (SM, SM, SM, VM) + (VM,) * GROUP + (HB,) * 5 + (VM,) * grp_count,
        [
            pltpu.VMEM((BEFORE * rows, width), f32),
            pltpu.VMEM((BEFORE * rows, width), bf16),
            pltpu.VMEM((BEFORE * rows, width), bf16),
            pltpu.VMEM((clusters, sets * quarter, rows), f32),
        ]
        + [pltpu.VMEM(*x) for x in shapes]
        + [pltpu.SemaphoreType.DMA((5,))],
        flops=200 * rows * rows * rows * 6,
    ))


def solution(mesh):
    in_specs = (
        P(AXES, None, None, None, None),
        P(AXES, None, None),
        P(AXES, None, None),
        P(AXES, None),
        P(),
        P(AXES, None),
        P(),
        P(),
    )
    out_specs = (P(AXES, None, None), P(AXES, None), P(None, "grp"))
    return jax.shard_map(
        per_device, mesh=mesh, in_specs=in_specs, out_specs=out_specs, check_vma=False
    )
```

```python
import functools

import jax
import jax.numpy as jnp
from jax import lax
from jax.experimental import pallas as pl
from jax.experimental.pallas import tpu as pltpu
from jax.sharding import PartitionSpec as P


TOUCH = 6
BAND = 8
FRONT = 4
BEFORE = BAND - 1
WINDOW = 2 * BAND - 2 + FRONT
PAIRS = TOUCH * (TOUCH + 1) // 2
GROUP = 8
SPAN = 2 * BAND - 1
STRIP = 8
AXES = ("pts", "grp")
VM = pltpu.VMEM
SM = pltpu.SMEM


def spec(space):
    return pl.BlockSpec(memory_space=space)


def size_of(shape, dtype):
    total = jnp.dtype(dtype).itemsize
    for extent in shape:
        total *= extent
    return total


def call(kernel, out_shapes, args, spaces, scratch=(), flops=0):
    moved = sum(size_of(x.shape, x.dtype) for x, s in zip(args, spaces) if s is VM)
    moved += sum(size_of(x.shape, x.dtype) for x in jax.tree.leaves(out_shapes))
    kept = 0
    for x in scratch:
        if x.memory_space is VM:
            kept += size_of(x.shape, x.dtype)
    limit = min(moved + kept + (8 << 20), 60 << 20)
    return pl.pallas_call(
        kernel,
        out_shape=out_shapes,
        in_specs=[spec(s) for s in spaces],
        out_specs=[spec(VM)] * len(out_shapes),
        scratch_shapes=list(scratch),
        cost_estimate=pl.CostEstimate(flops=flops, bytes_accessed=moved, transcendentals=0),
        compiler_params=pltpu.CompilerParams(vmem_limit_bytes=limit),
    )(*args)


NT = (((1,), (1,)), ((), ()))
TN = (((0,), (0,)), ((), ()))
NN = (((1,), (0,)), ((), ()))


def product(a, b, dims):
    return lax.dot_general(a, b, dims, preferred_element_type=jnp.float32)


def halves(x):
    high = x.astype(jnp.bfloat16)
    return high, (x - high.astype(jnp.float32)).astype(jnp.bfloat16)


def product3(a, b, dims):
    return (
        product(a[0], b[0], dims) + product(a[0], b[1], dims) + product(a[1], b[0], dims)
    )


def pair_index(a, b):
    return (TOUCH - 1) * a - (a * (a - 1)) // 2 + b


def pair_kernel(dims, meta, incidence, jac, blocks, grad, cam, *refs):
    rows, points, piece, grp_count, clusters = dims
    outs, (out, scaled, plain, rhs, pulls) = refs[:GROUP], refs[GROUP:]
    slots = [lax.rem(incidence[0, k] + clusters - meta[2], clusters) for k in range(TOUCH)]
    ranks = [
        sum((slots[m] < slots[k]).astype(jnp.int32) for m in range(TOUCH) if m != k)
        for k in range(TOUCH)
    ]
    v00, v11, v22 = blocks[0:1, :], blocks[1:2, :], blocks[2:3, :]
    v01, v02, v12 = blocks[3:4, :], blocks[4:5, :], blocks[5:6, :]
    a00 = v11 * v22 - v12 * v12
    a11 = v00 * v22 - v02 * v02
    a22 = v00 * v11 - v01 * v01
    a01 = v02 * v12 - v01 * v22
    a02 = v01 * v12 - v11 * v02
    a12 = v01 * v02 - v00 * v12
    inv = 1.0 / (v00 * a00 + v01 * a01 + v02 * a02)
    vinv = [
        [a00 * inv, a01 * inv, a02 * inv],
        [a01 * inv, a11 * inv, a12 * inv],
        [a02 * inv, a12 * inv, a22 * inv],
    ]
    rhs[...] = jnp.zeros_like(rhs)
    rhs[0:1, :] = cam[...]
    wide_grad = grad[...].astype(jnp.float32)
    for c in range(3):
        pulls[:, c * points : (c + 1) * points] = jnp.broadcast_to(
            wide_grad[c : c + 1, :], (16, points)
        ).astype(jnp.bfloat16)
    for a in range(TOUCH):
        k = sum(jnp.where(ranks[m] == a, m, 0) for m in range(TOUCH))
        t = sum(jnp.where(ranks[m] == a, slots[m], 0) for m in range(TOUCH))
        parts = [jac[c, k] for c in range(3)]
        wide = [x.astype(jnp.float32) for x in parts]
        for c in range(3):
            total = wide[0] * vinv[0][c] + wide[1] * vinv[1][c] + wide[2] * vinv[2][c]
            scaled[a, :, c * points : (c + 1) * points] = total.astype(jnp.bfloat16)
            plain[a * rows : (a + 1) * rows, c * points : (c + 1) * points] = parts[c]
        pulled = product(pulls[...], scaled[a], NT)
        rhs[pl.ds(t, 1), :] = rhs[pl.ds(t, 1), :] - pulled[0:1, :]
    for a in range(TOUCH):
        tiles = product(scaled[a], plain[a * rows : TOUCH * rows, :], NT)
        for b in range(a, TOUCH):
            at = pair_index(a, b) * piece
            for e in range(GROUP):
                first = (e % grp_count) * (rows // grp_count) + (e // grp_count) * piece
                out[e, at : at + piece, :] = tiles[
                    first : first + piece, (b - a) * rows : (b - a + 1) * rows
                ]
    lane = lax.broadcasted_iota(jnp.int32, (BAND, rows), 1)
    early = lax.rem(lane // BAND, BAND)
    late = early + lax.rem(lane, BAND)
    ones = jnp.ones_like(lane)
    none = jnp.zeros_like(lane)
    less, less_late, hit, hit_late = none, none, none, none
    for k in range(TOUCH):
        less = less + jnp.where(early > slots[k], ones, none)
        less_late = less_late + jnp.where(late > slots[k], ones, none)
        hit = hit + jnp.where(early == slots[k], ones, none)
        hit_late = hit_late + jnp.where(late == slots[k], ones, none)
    pick = jnp.where(hit * hit_late > 0, pair_index(less, less_late), -1).astype(jnp.float32)
    tail = PAIRS * piece
    for e in range(GROUP):
        out[e, tail : tail + BAND, :] = rhs[...]
        out[e, tail + BAND : tail + 2 * BAND, :] = pick
    place = lax.rem(meta[2], GROUP)
    for bit in range(GROUP):
        outs[bit][...] = out[place ^ bit]


def merge_kernel(dims, owner, meta, *refs):
    piece, pts_count, capacity, sends = dims
    arrived, outs = refs[:GROUP], refs[GROUP : GROUP + sends]
    got, out, rhs, table, pick, sem = refs[GROUP + sends :]
    place = lax.rem(meta[2], GROUP)
    for bit in range(GROUP):
        got[place ^ bit] = arrived[bit][...]
    flip = meta[0] if sends > 1 else 0
    base = lax.rem(meta[2] // GROUP * (GROUP * BAND), pts_count)
    tail = PAIRS * piece
    for j in range(GROUP):
        row = got[j, tail + BAND : tail + 2 * BAND, :]
        table[j : j + 1, :] = row[0:1, :].astype(jnp.int32)
    copy = pltpu.make_async_copy(table, pick, sem)
    copy.start()
    copy.wait()
    for row in range(SPAN):
        for offset in range(BAND):
            if row + offset >= SPAN:
                continue
            total = None
            for j in range(GROUP):
                t = row - j
                if t < 0 or t + offset > BAND - 1:
                    continue
                at = pick[j, t * BAND + offset]
                start = pl.multiple_of(jnp.maximum(at, 0) * piece, piece)
                value = jnp.where(at >= 0, got[j, pl.ds(start, piece), :], 0.0)
                total = value if total is None else total + value
            relative = BAND * row + offset
            dest = owner[lax.rem(base + relative, pts_count)]
            slot = relative // pts_count
            out[dest ^ flip, slot * piece : (slot + 1) * piece, :] = total
    rhs[...] = jnp.zeros_like(rhs)
    for j in range(GROUP):
        rhs[j : j + BAND, :] = rhs[j : j + BAND, :] + got[j, PAIRS * piece : PAIRS * piece + BAND, :]
    for dest in range(pts_count):
        out[dest, capacity * piece : capacity * piece + 2 * BAND, :] = rhs[...]
    for bit in range(sends):
        outs[bit][...] = out[bit] if sends > 1 else out[...]


def residue_of(owner, meta, pts_count):
    return sum(jnp.where(owner[i] == meta[0], i, 0) for i in range(pts_count))


def owner_kernel(
    dims, owner, meta, front, damping, *refs
):
    piece, pts_count, capacity, grp_count, quarter, clusters, sets, sends = dims
    arrived = refs[:sends]
    outs = refs[sends : sends + grp_count]
    direct, mirror, reduced, got, rows_out = refs[sends + grp_count :]
    for bit in range(sends):
        if sends > 1:
            got[meta[0] ^ bit] = arrived[bit][...]
        else:
            got[...] = arrived[0][...]
    residue, my_grp, start = residue_of(owner, meta, pts_count), meta[1], front[0]
    members = GROUP // grp_count
    planes = clusters // GROUP
    cols = rows_out.shape[3]
    offset = lax.rem(residue, BAND)
    part = residue // BAND
    stride = pts_count // BAND
    diag = (
        lax.broadcasted_iota(jnp.int32, (quarter, cols), 0) + my_grp * quarter
        == lax.broadcasted_iota(jnp.int32, (quarter, cols), 1)
    )
    diag = diag & (offset == 0)
    for m in range(BAND * grp_count):
        home = (residue + pts_count * m) // BAND
        plane = home // GROUP
        row = lax.rem(home, GROUP)
        before = lax.rem(plane + planes - 1, planes)
        near = (BAND * row + offset) // pts_count
        far = (BAND * (row + GROUP) + offset) // pts_count
        has_far = row + GROUP + offset < SPAN
        far = jnp.where(has_far, far, 0)
        for y in range(members):
            value = got[plane * members + y, pl.ds(pl.multiple_of(near * piece, piece), piece), :]
            extra = got[before * members + y, pl.ds(pl.multiple_of(far * piece, piece), piece), :]
            total = value + jnp.where(has_far, extra, 0.0)
            part_diag = diag[y * piece : (y + 1) * piece, :]
            total = total + jnp.where(part_diag, damping[pl.ds(home, 1), :], 0.0)
            rows_out[(m // BAND) ^ my_grp, m % BAND, y * piece : (y + 1) * piece, :] = total
    for i in range(sets):
        j = lax.rem(part + 2 * clusters - start, stride) + stride * i
        home = lax.rem(start + jnp.minimum(j, FRONT - 1), clusters)
        at = (BAND * home + offset) // pts_count
        value = rows_out[(at // BAND) ^ my_grp, lax.rem(at, BAND)]
        j = lax.rem(part + 2 * clusters - start + offset, stride) + stride * i
        home = lax.rem(start + jnp.minimum(j, FRONT - 1) + clusters - offset, clusters)
        at = (BAND * home + offset) // pts_count
        other = rows_out[(at // BAND) ^ my_grp, lax.rem(at, BAND)]
        for layer in range(direct.shape[0] // (sets * quarter)):
            at = (layer * sets + i) * quarter
            direct[at : at + quarter, :] = value
            mirror[at : at + quarter, :] = other
    for bit in range(grp_count):
        for i in range(BAND):
            outs[bit][i * quarter : (i + 1) * quarter, :] = rows_out[bit, i]
    tail = capacity * piece
    for plane in range(planes):
        before = (plane + planes - 1) % planes
        reduced[plane * GROUP : (plane + 1) * GROUP, :] = (
            got[plane * members, tail : tail + BAND, :]
            + got[before * members, tail + BAND : tail + 2 * BAND, :]
        )


def gather(gathered, sides, meta, clusters, ring):
    layers = clusters // GROUP
    place, level = lax.rem(meta[2], GROUP), meta[2] // GROUP
    for i in range(GROUP // 2):
        for z in range(layers):
            at = lax.rem(level + layers - z, layers) if ring else z
            at = at * GROUP + (place ^ (2 * i))
            count = gathered.shape[1]
            ref, first = sides[i]
            gathered[at] = ref[first + z * count : first + (z + 1) * count, :]
            ref, first = sides[GROUP // 2 + i]
            gathered[at ^ 1] = ref[first + z * count : first + (z + 1) * count, :]


def fetch(gathered, owner, tile, slot, dims):
    pts_count, grp_count, quarter = dims
    source = owner[lax.rem(tile, pts_count)] * grp_count
    rows = slice(slot * quarter, (slot + 1) * quarter)
    return jnp.concatenate([gathered[source + g, rows, :] for g in range(grp_count)], axis=0)


def factor_kernel(dims, meta, front, owner, reduced, *refs):
    pts_count, grp_count, quarter, clusters, ring = dims
    sides = [(ref, 0) for ref in refs[:GROUP]]
    tail_out, solve_high, solve_low, behind_high, behind_low = refs[GROUP : GROUP + 5]
    upper, behind, gathered, work, done, square, wide = refs[GROUP + 5 :]
    rows = done.shape[0]
    width = FRONT * rows
    start = front[0]
    stride = pts_count // BAND
    after = BAND - 1
    last = after * rows
    gather(gathered, sides, meta, clusters, ring)
    work[rows:, :] = jnp.zeros((STRIP, 2 * rows), jnp.float32)
    wide[...] = jnp.zeros_like(wide)
    upper[...] = jnp.zeros_like(upper)
    square[...] = jnp.zeros_like(square)
    row_id = lax.broadcasted_iota(jnp.int32, (rows, 1), 0)
    col_id = lax.broadcasted_iota(jnp.int32, (1, rows), 1)
    eye = (row_id == col_id).astype(jnp.float32)
    for j in range(FRONT):
        home = lax.rem(start + j, clusters)
        for e in range(BAND):
            tile = fetch(
                gathered, owner, BAND * home + e, j // stride, (pts_count, grp_count, quarter)
            )
            if j + e < FRONT:
                if e == 0:
                    tile = 0.5 * (tile + tile.T)
                square[j, :, (j + e) * rows : (j + e + 1) * rows] = tile
            else:
                at = (j + e - FRONT) * rows
                wide[at : at + rows, j * rows : (j + 1) * rows] = tile.T
        wide[last : last + 1, j * rows : (j + 1) * rows] = reduced[pl.ds(home, 1), :]
    for j in range(FRONT):
        here = j * rows
        work[0:rows, 0:rows] = square[j, :, here : here + rows]
        work[0:rows, rows : 2 * rows] = eye
        eliminate(work, done, rows)
        inverse = jnp.where(row_id >= col_id, done[:, rows : 2 * rows], 0.0)
        pair = halves(inverse)
        upper[j, :, here : here + rows] = jnp.where(row_id <= col_id, done[:, 0:rows], 0.0)
        parts = []
        if j < FRONT - 1:
            parts.append(square[j, :, here + rows : width])
        if j > 0:
            parts.append(square[j, :, width : width + here])
        line = product3(pair, halves(jnp.concatenate(parts, axis=1)), NN)
        ahead = width - here - rows
        if ahead:
            upper[j, :, here + rows :] = line[:, 0:ahead]
        solve = jnp.concatenate([line[:, ahead:], inverse], axis=1) if j else inverse
        high, low = halves(solve)
        solve_high[here : here + rows, 0 : here + rows] = high
        solve_low[here : here + rows, 0 : here + rows] = low
        if j < FRONT - 1:
            zero = jnp.zeros((rows, ahead), jnp.bfloat16)
            solve_high[here : here + rows, here + rows :] = zero
            solve_low[here : here + rows, here + rows :] = zero
            both = halves(line[:, 0:ahead])
            for i in range(j + 1, FRONT):
                skip = (i - j - 1) * rows
                left = tuple(x[:, skip : skip + rows] for x in both)
                right = tuple(
                    jnp.concatenate([x[:, skip:], y], axis=1) for x, y in zip(both, (high, low))
                )
                change = product3(left, right, TN)
                cut = width - i * rows
                square[i, :, i * rows : width] = square[i, :, i * rows : width] - change[:, 0:cut]
                square[i, :, width : width + here + rows] = (
                    square[i, :, width : width + here + rows] - change[:, cut:]
                )
    result = solve_rows(wide, solve_high, solve_low)
    high, low = halves(result)
    behind_high[...] = high
    behind_low[...] = low
    behind[...] = result
    first = pl.ds(pl.multiple_of(meta[1] * rows, rows), rows)
    for j in range(FRONT):
        tail_out[j * rows : (j + 1) * rows, :] = upper[meta[1], :, j * rows : (j + 1) * rows].T
    tail_out[FRONT * rows : FRONT * rows + last, :] = behind[0:last, first]
    for j in range(FRONT):
        at = FRONT * rows + last + 8 * j
        tail_out[at : at + 8, :] = result[last : last + 8, j * rows : (j + 1) * rows]


def eliminate(work, done, rows):
    lanes = lax.broadcasted_iota(jnp.int32, (STRIP, rows), 1)
    subs = lax.broadcasted_iota(jnp.int32, (STRIP, rows), 0)

    def strip(p, carry):
        now, past = carry
        at = pl.multiple_of(p * STRIP, STRIP)
        lhs = jnp.where(lanes >= at + STRIP, past[:, 0:rows], 0.0)
        work[0:rows, :] = work[0:rows, :] - product3(halves(lhs), halves(past), TN)
        ahead = work[pl.ds(at + STRIP, STRIP), :]
        now_a, now_i = now[:, 0:rows], now[:, rows : 2 * rows]
        next_a, next_i = ahead[:, 0:rows], ahead[:, rows : 2 * rows]
        shift = lax.rem(rows - at, rows)
        turned = pltpu.roll(now_a, shift, 1)
        turned_next = pltpu.roll(next_a, shift, 1)
        column = [jnp.broadcast_to(turned[:, i : i + 1], (STRIP, rows)) for i in range(STRIP)]
        below = [jnp.broadcast_to(turned_next[:, i : i + 1], (STRIP, rows)) for i in range(STRIP)]
        norm = jnp.zeros((STRIP, rows), jnp.float32)

        def row(value, i):
            return jnp.broadcast_to(value[i : i + 1, :], (STRIP, rows))

        for i in range(0, STRIP, 2):
            a, b, c = row(column[i], i), row(column[i + 1], i), row(column[i + 1], i + 1)
            det = a * c - b * b
            inv = 1.0 / a
            inv_second = a * (1.0 / det)
            ratio = b * inv
            norm = jnp.where(subs == i, lax.rsqrt(a), norm)
            norm = jnp.where(subs == i + 1, lax.rsqrt(det * inv), norm)
            scale = jnp.where(subs > i, column[i] * inv, 0.0)
            scale_next = below[i] * inv
            second = jnp.where(subs > i + 1, (column[i + 1] - scale * b) * inv_second, 0.0)
            second_next = (below[i + 1] - scale_next * b) * inv_second
            for k in range(i + 2, STRIP):
                top = row(column[k], i)
                low = row(column[k], i + 1) - ratio * top
                column[k] = column[k] - scale * top - second * low
                below[k] = below[k] - scale_next * top - second_next * low
            line_a, line_i = row(now_a, i), row(now_i, i)
            low_a = row(now_a, i + 1) - ratio * line_a
            low_i = row(now_i, i + 1) - ratio * line_i
            now_a = now_a - scale * line_a - second * low_a
            now_i = now_i - scale * line_i - second * low_i
            next_a = next_a - scale_next * line_a - second_next * low_a
            next_i = next_i - scale_next * line_i - second_next * low_i
        finished = jnp.concatenate([now_a * norm, now_i * norm], axis=1)
        done[pl.ds(at, STRIP), :] = finished
        return (jnp.concatenate([next_a, next_i], axis=1), finished)

    first = work[0:STRIP, :]
    lax.fori_loop(0, rows // STRIP, strip, (first, jnp.zeros_like(first)))


def solve_rows(wide, solve_high, solve_low):
    half = solve_high.shape[0] // 2
    high, low = halves(wide[...])
    left = product3(
        (high[:, :half], low[:, :half]),
        (solve_high[:half, :half], solve_low[:half, :half]),
        NT,
    )
    right = product3((high, low), (solve_high[half:, :], solve_low[half:, :]), NT)
    return jnp.concatenate([left, right], axis=1)


def update_kernel(dims, meta, front, owner, reduced, *refs):
    pts_count, grp_count, quarter, clusters, ring = dims
    first, swapped, second, third, fourth, kept_chunk = refs[:6]
    refs = refs[6:]
    count = first.shape[0]
    chunk = BAND * quarter
    crossed = (second, third, fourth)
    sides = [(first, 0)] + [(ref, 0) for ref in crossed]
    sides += [(swapped, 0)] + [(ref, count) for ref in crossed]
    chunks = (
        (kept_chunk, 0), (swapped, count), (second, 2 * count), (second, 2 * count + chunk)
    )
    tail, solve_high, solve_low, behind_high, behind_low = refs[:5]
    tiles_out, rhs_out, panel_out, wide, ahead_high, ahead_low, gathered = refs[5:]
    rows = tiles_out.shape[1]
    residue, my_grp, start = residue_of(owner, meta, pts_count), meta[1], front[0]
    device = meta[2]
    stride = pts_count // BAND
    gather(gathered, sides, meta, clusters, ring)
    wide[...] = jnp.zeros_like(wide)
    for j in range(FRONT):
        for i in range(j, BEFORE):
            e = BEFORE + j - i
            home = lax.rem(start + j + clusters - e, clusters)
            tile = fetch(
                gathered, owner, BAND * home + e, j // stride, (pts_count, grp_count, quarter)
            )
            wide[i * rows : (i + 1) * rows, j * rows : (j + 1) * rows] = tile
    result = solve_rows(wide, solve_high, solve_low)
    wide[...] = result
    high, low = halves(result)
    ahead_high[...] = high
    ahead_low[...] = low
    first = pl.ds(pl.multiple_of(my_grp * rows, rows), rows)
    panel_out[0 : BEFORE * rows, :] = wide[:, first]
    panel_out[BEFORE * rows :, :] = tail[0 : (BEFORE + FRONT) * rows, :]
    base = start + clusters - BEFORE

    def ahead(position):
        at = pl.ds(pl.multiple_of(position * rows, rows), rows)
        return (ahead_high[at, :], ahead_low[at, :])

    def past(position):
        at = pl.ds(pl.multiple_of((position - BEFORE - FRONT) * rows, rows), rows)
        return (behind_high[at, :], behind_low[at, :])

    def is_ahead(position):
        return position < BEFORE

    def is_past(position):
        return (position < WINDOW) & (position >= BEFORE + FRONT)

    for i in range(BAND):
        tile = residue + pts_count * (BAND * my_grp + i)
        home = tile // BAND
        offset = lax.rem(tile, BAND)
        one = lax.rem(home + 2 * clusters - base, clusters)
        two = lax.rem(home + offset + 2 * clusters - base, clusters)
        for bit in range(grp_count):
            at = pl.multiple_of((my_grp ^ bit) * quarter, quarter)
            ref, begin = chunks[bit]
            begin = begin + i * quarter
            tiles_out[i, pl.ds(at, quarter), :] = ref[begin : begin + quarter, :]
        for left, right, test_left, test_right in (
            (ahead, ahead, is_ahead, is_ahead),
            (ahead, past, is_ahead, is_past),
            (past, past, is_past, is_past),
        ):
            @pl.when(test_left(one) & test_right(two))
            def _():
                tiles_out[i] = tiles_out[i] - product3(left(one), right(two), NT)

    position = lax.rem(device + 2 * clusters - base, clusters)
    mine = reduced[pl.ds(device, 1), :]
    rhs_out[...] = mine
    last = (BEFORE + FRONT) * rows
    front_row = [tail[last + 8 * j : last + 8 * j + 8, :] for j in range(FRONT)]
    for take, test in ((ahead, is_ahead), (past, is_past)):
        @pl.when(test(position))
        def _():
            known = halves(jnp.concatenate(front_row, axis=1))
            rhs_out[...] = mine - product3(known, take(position), NT)[0:1, :]

    @pl.when((position >= BEFORE) & (position < BEFORE + FRONT))
    def _():
        at = pl.multiple_of(last + 8 * (position - BEFORE), 8)
        rhs_out[...] = tail[pl.ds(at, 8), :][0:1, :]


def per_device(
    jacobian, point_blocks, point_grad, camera_grad, damping, incidence, tile_owner, front_first
):
    pts_count = lax.axis_size("pts")
    grp_count = lax.axis_size("grp")
    clusters = pts_count * grp_count
    my_grp = lax.axis_index("grp")
    my_pts = lax.axis_index("pts")
    device = my_pts * grp_count + my_grp
    rows = jacobian.shape[2]
    points = jacobian.shape[4]
    piece = rows // GROUP
    quarter = rows // grp_count
    capacity = (BAND * (SPAN - 1)) // pts_count + 1
    stride = pts_count // BAND
    sets = -(-FRONT // stride)
    f32 = jnp.float32
    layers = clusters // GROUP
    columns = [[GROUP * z + e for z in range(layers)] for e in range(GROUP)]
    swap = [(i, i ^ 1) for i in range(clusters)]

    def flip(values, axis, count):
        moved = [
            lax.ppermute(value, axis, [(p, p ^ (bit + 1)) for p in range(count)])
            for bit, value in enumerate(values[1:])
        ]
        return [values[0], *moved]

    def exchange(value, lists):
        return lax.all_to_all(
            value, AXES, split_axis=0, concat_axis=0, tiled=True, axis_index_groups=lists
        )

    lane = jnp.arange(8)
    meta = jnp.where(lane == 0, my_pts, jnp.where(lane == 1, my_grp, device)).astype(jnp.int32)
    bf16 = jnp.bfloat16
    jac = jnp.transpose(jacobian[0], (2, 0, 1, 3))
    block_rows = PAIRS * piece + 2 * BAND
    sent = call(
        functools.partial(pair_kernel, (rows, points, piece, grp_count, clusters)),
        [jax.ShapeDtypeStruct((block_rows, rows), f32)] * GROUP,
        (meta, incidence, jac, point_blocks[0], point_grad[0], camera_grad),
        (SM, SM, VM, VM, VM, VM),
        (
            pltpu.VMEM((GROUP, block_rows, rows), f32),
            pltpu.VMEM((TOUCH, rows, 3 * points), bf16),
            pltpu.VMEM((TOUCH * rows, 3 * points), bf16),
            pltpu.VMEM((BAND, rows), f32),
            pltpu.VMEM((16, 3 * points), bf16),
        ),
        flops=2 * PAIRS * rows * rows * 3 * points,
    )
    got = flip(sent, AXES, clusters)
    sends = pts_count if pts_count <= GROUP else 1
    send_rows = capacity * piece + 2 * BAND
    shape = (send_rows, rows) if sends > 1 else (pts_count, send_rows, rows)
    sent = call(
        functools.partial(merge_kernel, (piece, pts_count, capacity, sends)),
        [jax.ShapeDtypeStruct(shape, f32)] * sends,
        (tile_owner, meta, *got),
        (SM, SM) + (VM,) * GROUP,
        (
            pltpu.VMEM((GROUP, block_rows, rows), f32),
            pltpu.VMEM((pts_count, send_rows, rows), f32),
            pltpu.VMEM((2 * BAND, rows), f32),
            pltpu.VMEM((GROUP, rows), jnp.int32),
            pltpu.SMEM((GROUP, rows), jnp.int32),
            pltpu.SemaphoreType.DMA(()),
        ),
    )
    if sends > 1:
        got = flip(sent, "pts", pts_count)
    else:
        got = [lax.all_to_all(sent[0], "pts", split_axis=0, concat_axis=0, tiled=True)]
    copies = layers if layers > 4 else 1
    *chunks, direct, mirror, reduced = call(
        functools.partial(
            owner_kernel,
            (piece, pts_count, capacity, grp_count, quarter, clusters, sets, sends),
        ),
        [jax.ShapeDtypeStruct((BAND * quarter, rows), f32)] * grp_count
        + [
            jax.ShapeDtypeStruct((copies * sets * quarter, rows), f32),
            jax.ShapeDtypeStruct((copies * sets * quarter, rows), f32),
            jax.ShapeDtypeStruct((clusters, rows), f32),
        ],
        (tile_owner, meta, front_first, damping, *got),
        (SM, SM, SM, VM) + (VM,) * sends,
        (
            pltpu.VMEM((pts_count, send_rows, rows), f32),
            pltpu.VMEM((grp_count, BAND, quarter, rows), f32),
        ),
    )
    ring = layers <= 4

    def along(value):
        if not ring:
            return exchange(value, columns)
        moved = []
        for z in range(1, layers):
            pairs = [(p, (p + GROUP * z) % clusters) for p in range(clusters)]
            moved.append(lax.ppermute(value, AXES, pairs))
        return jnp.concatenate([value, *moved])

    def across(values):
        moved = []
        for i, value in enumerate(values):
            pairs = [(p, p ^ (2 * i + 2)) for p in range(clusters)]
            moved.append(lax.ppermute(value, AXES, pairs))
        return moved

    direct = along(direct)
    direct, mirror, *chunks = lax.optimization_barrier((direct, mirror, *chunks))
    mine = [direct, *across([direct] * 3)]
    theirs = [lax.ppermute(direct, AXES, swap)]
    mirror = along(mirror)
    swapped = lax.ppermute(jnp.concatenate([mirror, chunks[1], chunks[3]]), AXES, swap)
    count = mirror.shape[0]
    chunk = BAND * quarter
    both = jnp.concatenate([mirror, swapped[:count]])
    more = jnp.concatenate([both, chunks[2], swapped[count + chunk :]])
    both, more, *mine = lax.optimization_barrier((both, more, *mine))
    theirs += [lax.ppermute(x, AXES, swap) for x in mine[1:]]
    sides = [mirror, swapped, *across([more, both, both]), chunks[0]]

    width = FRONT * rows
    dims = (pts_count, grp_count, quarter, clusters)
    tall = BEFORE * rows + 8
    tail = (FRONT + BEFORE) * rows + 8 * FRONT
    shapes = (
        ((tail, rows), f32),
        ((width, width), bf16),
        ((width, width), bf16),
        ((tall, width), bf16),
        ((tall, width), bf16),
    )
    stored = call(
        functools.partial(factor_kernel, dims + (ring,)),
        [jax.ShapeDtypeStruct(*x) for x in shapes],
        (meta, front_first, tile_owner, reduced, *mine, *theirs),
        (SM, SM, SM, VM) + (VM,) * GROUP,
        [
            pltpu.VMEM((FRONT, rows, width), f32),
            pltpu.VMEM((tall, width), f32),
            pltpu.VMEM((clusters, sets * quarter, rows), f32),
            pltpu.VMEM((rows + STRIP, 2 * rows), f32),
            pltpu.VMEM((rows, 2 * rows), f32),
            pltpu.VMEM((FRONT, rows, 2 * width), f32),
            pltpu.VMEM((tall, width), f32),
        ],
        flops=400 * rows * rows * rows * 6,
    )
    return tuple(call(
        functools.partial(update_kernel, dims + (ring,)),
        [
            jax.ShapeDtypeStruct((BAND, rows, rows), f32),
            jax.ShapeDtypeStruct((1, rows), f32),
            jax.ShapeDtypeStruct((WINDOW * rows, rows), f32),
        ],
        (meta, front_first, tile_owner, reduced, *sides, *stored),
        (SM, SM, SM, VM) + (VM,) * 11,
        [
            pltpu.VMEM((BEFORE * rows, width), f32),
            pltpu.VMEM((BEFORE * rows, width), bf16),
            pltpu.VMEM((BEFORE * rows, width), bf16),
            pltpu.VMEM((clusters, sets * quarter, rows), f32),
        ],
        flops=200 * rows * rows * rows * 6,
    ))


def solution(mesh):
    in_specs = (
        P(AXES, None, None, None, None),
        P(AXES, None, None),
        P(AXES, None, None),
        P(AXES, None),
        P(),
        P(AXES, None),
        P(),
        P(),
    )
    out_specs = (P(AXES, None, None), P(AXES, None), P(None, "grp"))

    return jax.shard_map(per_device, mesh=mesh, in_specs=in_specs, out_specs=out_specs, check_vma=False)
```

```python
import functools

import jax
import jax.numpy as jnp
from jax import lax
from jax.experimental import pallas as pl
from jax.experimental.pallas import tpu as pltpu
from jax.sharding import PartitionSpec as P


TOUCH = 6
BAND = 8
FRONT = 4
BEFORE = BAND - 1
WINDOW = 2 * BAND - 2 + FRONT
PAIRS = TOUCH * (TOUCH + 1) // 2
GROUP = 8
SPAN = 2 * BAND - 1
STRIP = 8
AXES = ("pts", "grp")
VM = pltpu.VMEM
SM = pltpu.SMEM


def spec(space):
    return pl.BlockSpec(memory_space=space)


def size_of(shape, dtype):
    total = jnp.dtype(dtype).itemsize
    for extent in shape:
        total *= extent
    return total


def call(kernel, out_shapes, args, spaces, scratch=(), flops=0):
    moved = sum(size_of(x.shape, x.dtype) for x, s in zip(args, spaces) if s is VM)
    moved += sum(size_of(x.shape, x.dtype) for x in jax.tree.leaves(out_shapes))
    kept = 0
    for x in scratch:
        if x.memory_space is VM:
            kept += size_of(x.shape, x.dtype)
    limit = min(moved + kept + (8 << 20), 60 << 20)
    return pl.pallas_call(
        kernel,
        out_shape=out_shapes,
        in_specs=[spec(s) for s in spaces],
        out_specs=[spec(VM)] * len(out_shapes),
        scratch_shapes=list(scratch),
        cost_estimate=pl.CostEstimate(flops=flops, bytes_accessed=moved, transcendentals=0),
        compiler_params=pltpu.CompilerParams(vmem_limit_bytes=limit),
    )(*args)


NT = (((1,), (1,)), ((), ()))
TN = (((0,), (0,)), ((), ()))
NN = (((1,), (0,)), ((), ()))


def product(a, b, dims):
    return lax.dot_general(a, b, dims, preferred_element_type=jnp.float32)


def halves(x):
    high = x.astype(jnp.bfloat16)
    return high, (x - high.astype(jnp.float32)).astype(jnp.bfloat16)


def product3(a, b, dims):
    return (
        product(a[0], b[0], dims) + product(a[0], b[1], dims) + product(a[1], b[0], dims)
    )


def pair_index(a, b):
    return (TOUCH - 1) * a - (a * (a - 1)) // 2 + b


def pair_kernel(dims, meta, incidence, jac, blocks, grad, cam, *refs):
    rows, points, piece, grp_count, clusters = dims
    outs, (out, scaled, plain, rhs, pulls) = refs[:GROUP], refs[GROUP:]
    slots = [lax.rem(incidence[0, k] + clusters - meta[2], clusters) for k in range(TOUCH)]
    ranks = [
        sum((slots[m] < slots[k]).astype(jnp.int32) for m in range(TOUCH) if m != k)
        for k in range(TOUCH)
    ]
    v00, v11, v22 = blocks[0:1, :], blocks[1:2, :], blocks[2:3, :]
    v01, v02, v12 = blocks[3:4, :], blocks[4:5, :], blocks[5:6, :]
    a00 = v11 * v22 - v12 * v12
    a11 = v00 * v22 - v02 * v02
    a22 = v00 * v11 - v01 * v01
    a01 = v02 * v12 - v01 * v22
    a02 = v01 * v12 - v11 * v02
    a12 = v01 * v02 - v00 * v12
    inv = 1.0 / (v00 * a00 + v01 * a01 + v02 * a02)
    vinv = [
        [a00 * inv, a01 * inv, a02 * inv],
        [a01 * inv, a11 * inv, a12 * inv],
        [a02 * inv, a12 * inv, a22 * inv],
    ]
    rhs[...] = jnp.zeros_like(rhs)
    rhs[0:1, :] = cam[...]
    wide_grad = grad[...].astype(jnp.float32)
    for c in range(3):
        pulls[:, c * points : (c + 1) * points] = jnp.broadcast_to(
            wide_grad[c : c + 1, :], (16, points)
        ).astype(jnp.bfloat16)
    for a in range(TOUCH):
        k = sum(jnp.where(ranks[m] == a, m, 0) for m in range(TOUCH))
        t = sum(jnp.where(ranks[m] == a, slots[m], 0) for m in range(TOUCH))
        parts = [jac[c, k] for c in range(3)]
        wide = [x.astype(jnp.float32) for x in parts]
        for c in range(3):
            total = wide[0] * vinv[0][c] + wide[1] * vinv[1][c] + wide[2] * vinv[2][c]
            scaled[a, :, c * points : (c + 1) * points] = total.astype(jnp.bfloat16)
            plain[a * rows : (a + 1) * rows, c * points : (c + 1) * points] = parts[c]
        pulled = product(pulls[...], scaled[a], NT)
        rhs[pl.ds(t, 1), :] = rhs[pl.ds(t, 1), :] - pulled[0:1, :]
    for a in range(TOUCH):
        tiles = product(scaled[a], plain[a * rows : TOUCH * rows, :], NT)
        for b in range(a, TOUCH):
            at = pair_index(a, b) * piece
            for e in range(GROUP):
                first = (e % grp_count) * (rows // grp_count) + (e // grp_count) * piece
                out[e, at : at + piece, :] = tiles[
                    first : first + piece, (b - a) * rows : (b - a + 1) * rows
                ]
    lane = lax.broadcasted_iota(jnp.int32, (BAND, rows), 1)
    early = lax.rem(lane // BAND, BAND)
    late = early + lax.rem(lane, BAND)
    ones = jnp.ones_like(lane)
    none = jnp.zeros_like(lane)
    less, less_late, hit, hit_late = none, none, none, none
    for k in range(TOUCH):
        less = less + jnp.where(early > slots[k], ones, none)
        less_late = less_late + jnp.where(late > slots[k], ones, none)
        hit = hit + jnp.where(early == slots[k], ones, none)
        hit_late = hit_late + jnp.where(late == slots[k], ones, none)
    pick = jnp.where(hit * hit_late > 0, pair_index(less, less_late), -1).astype(jnp.float32)
    tail = PAIRS * piece
    for e in range(GROUP):
        out[e, tail : tail + BAND, :] = rhs[...]
        out[e, tail + BAND : tail + 2 * BAND, :] = pick
    place = lax.rem(meta[2], GROUP)
    for bit in range(GROUP):
        outs[bit][...] = out[place ^ bit]


def merge_kernel(dims, owner, meta, *refs):
    piece, pts_count, capacity, sends = dims
    arrived, outs = refs[:GROUP], refs[GROUP : GROUP + sends]
    got, out, rhs, table, pick, sem = refs[GROUP + sends :]
    place = lax.rem(meta[2], GROUP)
    for bit in range(GROUP):
        got[place ^ bit] = arrived[bit][...]
    flip = meta[0] if sends > 1 else 0
    base = lax.rem(meta[2] // GROUP * (GROUP * BAND), pts_count)
    tail = PAIRS * piece
    for j in range(GROUP):
        row = got[j, tail + BAND : tail + 2 * BAND, :]
        table[j : j + 1, :] = row[0:1, :].astype(jnp.int32)
    copy = pltpu.make_async_copy(table, pick, sem)
    copy.start()
    copy.wait()
    for row in range(SPAN):
        for offset in range(BAND):
            if row + offset >= SPAN:
                continue
            total = None
            for j in range(GROUP):
                t = row - j
                if t < 0 or t + offset > BAND - 1:
                    continue
                at = pick[j, t * BAND + offset]
                start = pl.multiple_of(jnp.maximum(at, 0) * piece, piece)
                value = jnp.where(at >= 0, got[j, pl.ds(start, piece), :], 0.0)
                total = value if total is None else total + value
            relative = BAND * row + offset
            dest = owner[lax.rem(base + relative, pts_count)]
            slot = relative // pts_count
            out[dest ^ flip, slot * piece : (slot + 1) * piece, :] = total
    rhs[...] = jnp.zeros_like(rhs)
    for j in range(GROUP):
        rhs[j : j + BAND, :] = rhs[j : j + BAND, :] + got[j, PAIRS * piece : PAIRS * piece + BAND, :]
    for dest in range(pts_count):
        out[dest, capacity * piece : capacity * piece + 2 * BAND, :] = rhs[...]
    for bit in range(sends):
        outs[bit][...] = out[bit] if sends > 1 else out[...]


def residue_of(owner, meta, pts_count):
    return sum(jnp.where(owner[i] == meta[0], i, 0) for i in range(pts_count))


def owner_kernel(
    dims, owner, meta, front, damping, *refs
):
    piece, pts_count, capacity, grp_count, quarter, clusters, sets, sends = dims
    arrived = refs[:sends]
    outs = refs[sends : sends + grp_count]
    direct, mirror, reduced, got, rows_out = refs[sends + grp_count :]
    for bit in range(sends):
        if sends > 1:
            got[meta[0] ^ bit] = arrived[bit][...]
        else:
            got[...] = arrived[0][...]
    residue, my_grp, start = residue_of(owner, meta, pts_count), meta[1], front[0]
    members = GROUP // grp_count
    planes = clusters // GROUP
    cols = rows_out.shape[3]
    offset = lax.rem(residue, BAND)
    part = residue // BAND
    stride = pts_count // BAND
    diag = (
        lax.broadcasted_iota(jnp.int32, (quarter, cols), 0) + my_grp * quarter
        == lax.broadcasted_iota(jnp.int32, (quarter, cols), 1)
    )
    diag = diag & (offset == 0)
    for m in range(BAND * grp_count):
        home = (residue + pts_count * m) // BAND
        plane = home // GROUP
        row = lax.rem(home, GROUP)
        before = lax.rem(plane + planes - 1, planes)
        near = (BAND * row + offset) // pts_count
        far = (BAND * (row + GROUP) + offset) // pts_count
        has_far = row + GROUP + offset < SPAN
        far = jnp.where(has_far, far, 0)
        for y in range(members):
            value = got[plane * members + y, pl.ds(pl.multiple_of(near * piece, piece), piece), :]
            extra = got[before * members + y, pl.ds(pl.multiple_of(far * piece, piece), piece), :]
            total = value + jnp.where(has_far, extra, 0.0)
            part_diag = diag[y * piece : (y + 1) * piece, :]
            total = total + jnp.where(part_diag, damping[pl.ds(home, 1), :], 0.0)
            rows_out[(m // BAND) ^ my_grp, m % BAND, y * piece : (y + 1) * piece, :] = total
    for i in range(sets):
        j = lax.rem(part + 2 * clusters - start, stride) + stride * i
        home = lax.rem(start + jnp.minimum(j, FRONT - 1), clusters)
        at = (BAND * home + offset) // pts_count
        value = rows_out[(at // BAND) ^ my_grp, lax.rem(at, BAND)]
        j = lax.rem(part + 2 * clusters - start + offset, stride) + stride * i
        home = lax.rem(start + jnp.minimum(j, FRONT - 1) + clusters - offset, clusters)
        at = (BAND * home + offset) // pts_count
        other = rows_out[(at // BAND) ^ my_grp, lax.rem(at, BAND)]
        for layer in range(direct.shape[0] // (sets * quarter)):
            at = (layer * sets + i) * quarter
            direct[at : at + quarter, :] = value
            mirror[at : at + quarter, :] = other
    for bit in range(grp_count):
        for i in range(BAND):
            outs[bit][i * quarter : (i + 1) * quarter, :] = rows_out[bit, i]
    tail = capacity * piece
    for plane in range(planes):
        before = (plane + planes - 1) % planes
        reduced[plane * GROUP : (plane + 1) * GROUP, :] = (
            got[plane * members, tail : tail + BAND, :]
            + got[before * members, tail + BAND : tail + 2 * BAND, :]
        )


def gather(gathered, sides, meta, clusters, ring):
    layers = clusters // GROUP
    place, level = lax.rem(meta[2], GROUP), meta[2] // GROUP
    for i in range(GROUP // 2):
        for z in range(layers):
            at = lax.rem(level + layers - z, layers) if ring else z
            at = at * GROUP + (place ^ (2 * i))
            count = gathered.shape[1]
            ref, first = sides[i]
            gathered[at] = ref[first + z * count : first + (z + 1) * count, :]
            ref, first = sides[GROUP // 2 + i]
            gathered[at ^ 1] = ref[first + z * count : first + (z + 1) * count, :]


def fetch(gathered, owner, tile, slot, dims):
    pts_count, grp_count, quarter = dims
    source = owner[lax.rem(tile, pts_count)] * grp_count
    rows = slice(slot * quarter, (slot + 1) * quarter)
    return jnp.concatenate([gathered[source + g, rows, :] for g in range(grp_count)], axis=0)


def factor_kernel(dims, meta, front, owner, reduced, *refs):
    pts_count, grp_count, quarter, clusters, ring = dims
    sides = [(ref, 0) for ref in refs[:GROUP]]
    tail_out, solve_high, solve_low, behind_high, behind_low = refs[GROUP : GROUP + 5]
    upper, behind, gathered, work, done, square, wide = refs[GROUP + 5 :]
    rows = done.shape[0]
    width = FRONT * rows
    start = front[0]
    stride = pts_count // BAND
    after = BAND - 1
    last = after * rows
    gather(gathered, sides, meta, clusters, ring)
    work[rows:, :] = jnp.zeros((STRIP, 2 * rows), jnp.float32)
    wide[...] = jnp.zeros_like(wide)
    upper[...] = jnp.zeros_like(upper)
    square[...] = jnp.zeros_like(square)
    row_id = lax.broadcasted_iota(jnp.int32, (rows, 1), 0)
    col_id = lax.broadcasted_iota(jnp.int32, (1, rows), 1)
    eye = (row_id == col_id).astype(jnp.float32)
    for j in range(FRONT):
        home = lax.rem(start + j, clusters)
        for e in range(BAND):
            tile = fetch(
                gathered, owner, BAND * home + e, j // stride, (pts_count, grp_count, quarter)
            )
            if j + e < FRONT:
                if e == 0:
                    tile = 0.5 * (tile + tile.T)
                square[j, :, (j + e) * rows : (j + e + 1) * rows] = tile
            else:
                at = (j + e - FRONT) * rows
                wide[at : at + rows, j * rows : (j + 1) * rows] = tile.T
        wide[last : last + 1, j * rows : (j + 1) * rows] = reduced[pl.ds(home, 1), :]
    for j in range(FRONT):
        here = j * rows
        work[0:rows, 0:rows] = square[j, :, here : here + rows]
        work[0:rows, rows : 2 * rows] = eye
        eliminate(work, done, rows)
        inverse = jnp.where(row_id >= col_id, done[:, rows : 2 * rows], 0.0)
        pair = halves(inverse)
        upper[j, :, here : here + rows] = jnp.where(row_id <= col_id, done[:, 0:rows], 0.0)
        parts = []
        if j < FRONT - 1:
            parts.append(square[j, :, here + rows : width])
        if j > 0:
            parts.append(square[j, :, width : width + here])
        line = product3(pair, halves(jnp.concatenate(parts, axis=1)), NN)
        ahead = width - here - rows
        if ahead:
            upper[j, :, here + rows :] = line[:, 0:ahead]
        solve = jnp.concatenate([line[:, ahead:], inverse], axis=1) if j else inverse
        high, low = halves(solve)
        solve_high[here : here + rows, 0 : here + rows] = high
        solve_low[here : here + rows, 0 : here + rows] = low
        if j < FRONT - 1:
            zero = jnp.zeros((rows, ahead), jnp.bfloat16)
            solve_high[here : here + rows, here + rows :] = zero
            solve_low[here : here + rows, here + rows :] = zero
            both = halves(line[:, 0:ahead])
            for i in range(j + 1, FRONT):
                skip = (i - j - 1) * rows
                left = tuple(x[:, skip : skip + rows] for x in both)
                right = tuple(
                    jnp.concatenate([x[:, skip:], y], axis=1) for x, y in zip(both, (high, low))
                )
                change = product3(left, right, TN)
                cut = width - i * rows
                square[i, :, i * rows : width] = square[i, :, i * rows : width] - change[:, 0:cut]
                square[i, :, width : width + here + rows] = (
                    square[i, :, width : width + here + rows] - change[:, cut:]
                )
    result = solve_rows(wide, solve_high, solve_low)
    high, low = halves(result)
    behind_high[...] = high
    behind_low[...] = low
    behind[...] = result
    first = pl.ds(pl.multiple_of(meta[1] * rows, rows), rows)
    for j in range(FRONT):
        tail_out[j * rows : (j + 1) * rows, :] = upper[meta[1], :, j * rows : (j + 1) * rows].T
    tail_out[FRONT * rows : FRONT * rows + last, :] = behind[0:last, first]
    for j in range(FRONT):
        at = FRONT * rows + last + 8 * j
        tail_out[at : at + 8, :] = result[last : last + 8, j * rows : (j + 1) * rows]


def eliminate(work, done, rows):
    lanes = lax.broadcasted_iota(jnp.int32, (STRIP, rows), 1)
    subs = lax.broadcasted_iota(jnp.int32, (STRIP, rows), 0)

    def strip(p, carry):
        now, past = carry
        at = pl.multiple_of(p * STRIP, STRIP)
        lhs = jnp.where(lanes >= at + STRIP, past[:, 0:rows], 0.0)
        work[0:rows, :] = work[0:rows, :] - product3(halves(lhs), halves(past), TN)
        now_a, now_i = now[:, 0:rows], now[:, rows : 2 * rows]
        shift = lax.rem(rows - at, rows)
        turned = pltpu.roll(now_a, shift, 1)
        turned_next = turned.T[STRIP : 2 * STRIP, :]
        column = [jnp.broadcast_to(turned[:, i : i + 1], (STRIP, rows)) for i in range(STRIP)]
        below = [jnp.broadcast_to(turned_next[:, i : i + 1], (STRIP, rows)) for i in range(STRIP)]
        norm = jnp.zeros((STRIP, rows), jnp.float32)
        next_a, next_i = norm, norm

        def row(value, i):
            return jnp.broadcast_to(value[i : i + 1, :], (STRIP, rows))

        for i in range(0, STRIP, 2):
            a, b, c = row(column[i], i), row(column[i + 1], i), row(column[i + 1], i + 1)
            det = a * c - b * b
            inv = 1.0 / a
            inv_second = a * (1.0 / det)
            ratio = b * inv
            norm = jnp.where(subs == i, lax.rsqrt(a), norm)
            norm = jnp.where(subs == i + 1, lax.rsqrt(det * inv), norm)
            scale = jnp.where(subs > i, column[i] * inv, 0.0)
            scale_next = below[i] * inv
            second = jnp.where(subs > i + 1, (column[i + 1] - scale * b) * inv_second, 0.0)
            second_next = (below[i + 1] - scale_next * b) * inv_second
            for k in range(i + 2, STRIP):
                top = row(column[k], i)
                low = row(column[k], i + 1) - ratio * top
                column[k] = column[k] - scale * top - second * low
                below[k] = below[k] - scale_next * top - second_next * low
            line_a, line_i = row(now_a, i), row(now_i, i)
            low_a = row(now_a, i + 1) - ratio * line_a
            low_i = row(now_i, i + 1) - ratio * line_i
            now_a = now_a - scale * line_a - second * low_a
            now_i = now_i - scale * line_i - second * low_i
            next_a = next_a + (scale_next * line_a + second_next * low_a)
            next_i = next_i + (scale_next * line_i + second_next * low_i)
        finished = jnp.concatenate([now_a * norm, now_i * norm], axis=1)
        done[pl.ds(at, STRIP), :] = finished
        ahead = work[pl.ds(at + STRIP, STRIP), :]
        return (ahead - jnp.concatenate([next_a, next_i], axis=1), finished)

    first = work[0:STRIP, :]
    lax.fori_loop(0, rows // STRIP, strip, (first, jnp.zeros_like(first)))


def solve_rows(wide, solve_high, solve_low):
    half = solve_high.shape[0] // 2
    high, low = halves(wide[...])
    left = product3(
        (high[:, :half], low[:, :half]),
        (solve_high[:half, :half], solve_low[:half, :half]),
        NT,
    )
    right = product3((high, low), (solve_high[half:, :], solve_low[half:, :]), NT)
    return jnp.concatenate([left, right], axis=1)


def update_kernel(dims, meta, front, owner, reduced, *refs):
    pts_count, grp_count, quarter, clusters, ring = dims
    first, swapped, second, third, fourth, kept_chunk = refs[:6]
    refs = refs[6:]
    count = first.shape[0]
    chunk = BAND * quarter
    crossed = (second, third, fourth)
    sides = [(first, 0)] + [(ref, 0) for ref in crossed]
    sides += [(swapped, 0)] + [(ref, count) for ref in crossed]
    chunks = (
        (kept_chunk, 0), (swapped, count), (second, 2 * count), (second, 2 * count + chunk)
    )
    tail, solve_high, solve_low, behind_high, behind_low = refs[:5]
    tiles_out, rhs_out, panel_out, wide, ahead_high, ahead_low, gathered = refs[5:]
    rows = tiles_out.shape[1]
    residue, my_grp, start = residue_of(owner, meta, pts_count), meta[1], front[0]
    device = meta[2]
    stride = pts_count // BAND
    gather(gathered, sides, meta, clusters, ring)
    wide[...] = jnp.zeros_like(wide)
    for j in range(FRONT):
        for i in range(j, BEFORE):
            e = BEFORE + j - i
            home = lax.rem(start + j + clusters - e, clusters)
            tile = fetch(
                gathered, owner, BAND * home + e, j // stride, (pts_count, grp_count, quarter)
            )
            wide[i * rows : (i + 1) * rows, j * rows : (j + 1) * rows] = tile
    result = solve_rows(wide, solve_high, solve_low)
    wide[...] = result
    high, low = halves(result)
    ahead_high[...] = high
    ahead_low[...] = low
    first = pl.ds(pl.multiple_of(my_grp * rows, rows), rows)
    panel_out[0 : BEFORE * rows, :] = wide[:, first]
    panel_out[BEFORE * rows :, :] = tail[0 : (BEFORE + FRONT) * rows, :]
    base = start + clusters - BEFORE

    def ahead(position):
        at = pl.ds(pl.multiple_of(position * rows, rows), rows)
        return (ahead_high[at, :], ahead_low[at, :])

    def past(position):
        at = pl.ds(pl.multiple_of((position - BEFORE - FRONT) * rows, rows), rows)
        return (behind_high[at, :], behind_low[at, :])

    def is_ahead(position):
        return position < BEFORE

    def is_past(position):
        return (position < WINDOW) & (position >= BEFORE + FRONT)

    for i in range(BAND):
        tile = residue + pts_count * (BAND * my_grp + i)
        home = tile // BAND
        offset = lax.rem(tile, BAND)
        one = lax.rem(home + 2 * clusters - base, clusters)
        two = lax.rem(home + offset + 2 * clusters - base, clusters)
        for bit in range(grp_count):
            at = pl.multiple_of((my_grp ^ bit) * quarter, quarter)
            ref, begin = chunks[bit]
            begin = begin + i * quarter
            tiles_out[i, pl.ds(at, quarter), :] = ref[begin : begin + quarter, :]
        for left, right, test_left, test_right in (
            (ahead, ahead, is_ahead, is_ahead),
            (ahead, past, is_ahead, is_past),
            (past, past, is_past, is_past),
        ):
            @pl.when(test_left(one) & test_right(two))
            def _():
                tiles_out[i] = tiles_out[i] - product3(left(one), right(two), NT)

    position = lax.rem(device + 2 * clusters - base, clusters)
    mine = reduced[pl.ds(device, 1), :]
    rhs_out[...] = mine
    last = (BEFORE + FRONT) * rows
    front_row = [tail[last + 8 * j : last + 8 * j + 8, :] for j in range(FRONT)]
    for take, test in ((ahead, is_ahead), (past, is_past)):
        @pl.when(test(position))
        def _():
            known = halves(jnp.concatenate(front_row, axis=1))
            rhs_out[...] = mine - product3(known, take(position), NT)[0:1, :]

    @pl.when((position >= BEFORE) & (position < BEFORE + FRONT))
    def _():
        at = pl.multiple_of(last + 8 * (position - BEFORE), 8)
        rhs_out[...] = tail[pl.ds(at, 8), :][0:1, :]


def per_device(
    jacobian, point_blocks, point_grad, camera_grad, damping, incidence, tile_owner, front_first
):
    pts_count = lax.axis_size("pts")
    grp_count = lax.axis_size("grp")
    clusters = pts_count * grp_count
    my_grp = lax.axis_index("grp")
    my_pts = lax.axis_index("pts")
    device = my_pts * grp_count + my_grp
    rows = jacobian.shape[2]
    points = jacobian.shape[4]
    piece = rows // GROUP
    quarter = rows // grp_count
    capacity = (BAND * (SPAN - 1)) // pts_count + 1
    stride = pts_count // BAND
    sets = -(-FRONT // stride)
    f32 = jnp.float32
    layers = clusters // GROUP
    columns = [[GROUP * z + e for z in range(layers)] for e in range(GROUP)]
    swap = [(i, i ^ 1) for i in range(clusters)]

    def flip(values, axis, count):
        moved = [
            lax.ppermute(value, axis, [(p, p ^ (bit + 1)) for p in range(count)])
            for bit, value in enumerate(values[1:])
        ]
        return [values[0], *moved]

    def exchange(value, lists):
        return lax.all_to_all(
            value, AXES, split_axis=0, concat_axis=0, tiled=True, axis_index_groups=lists
        )

    lane = jnp.arange(8)
    meta = jnp.where(lane == 0, my_pts, jnp.where(lane == 1, my_grp, device)).astype(jnp.int32)
    bf16 = jnp.bfloat16
    jac = jnp.transpose(jacobian[0], (2, 0, 1, 3))
    block_rows = PAIRS * piece + 2 * BAND
    sent = call(
        functools.partial(pair_kernel, (rows, points, piece, grp_count, clusters)),
        [jax.ShapeDtypeStruct((block_rows, rows), f32)] * GROUP,
        (meta, incidence, jac, point_blocks[0], point_grad[0], camera_grad),
        (SM, SM, VM, VM, VM, VM),
        (
            pltpu.VMEM((GROUP, block_rows, rows), f32),
            pltpu.VMEM((TOUCH, rows, 3 * points), bf16),
            pltpu.VMEM((TOUCH * rows, 3 * points), bf16),
            pltpu.VMEM((BAND, rows), f32),
            pltpu.VMEM((16, 3 * points), bf16),
        ),
        flops=2 * PAIRS * rows * rows * 3 * points,
    )
    got = flip(sent, AXES, clusters)
    sends = pts_count if pts_count <= GROUP else 1
    send_rows = capacity * piece + 2 * BAND
    shape = (send_rows, rows) if sends > 1 else (pts_count, send_rows, rows)
    sent = call(
        functools.partial(merge_kernel, (piece, pts_count, capacity, sends)),
        [jax.ShapeDtypeStruct(shape, f32)] * sends,
        (tile_owner, meta, *got),
        (SM, SM) + (VM,) * GROUP,
        (
            pltpu.VMEM((GROUP, block_rows, rows), f32),
            pltpu.VMEM((pts_count, send_rows, rows), f32),
            pltpu.VMEM((2 * BAND, rows), f32),
            pltpu.VMEM((GROUP, rows), jnp.int32),
            pltpu.SMEM((GROUP, rows), jnp.int32),
            pltpu.SemaphoreType.DMA(()),
        ),
    )
    if sends > 1:
        got = flip(sent, "pts", pts_count)
    else:
        got = [lax.all_to_all(sent[0], "pts", split_axis=0, concat_axis=0, tiled=True)]
    copies = layers if layers > 4 else 1
    *chunks, direct, mirror, reduced = call(
        functools.partial(
            owner_kernel,
            (piece, pts_count, capacity, grp_count, quarter, clusters, sets, sends),
        ),
        [jax.ShapeDtypeStruct((BAND * quarter, rows), f32)] * grp_count
        + [
            jax.ShapeDtypeStruct((copies * sets * quarter, rows), f32),
            jax.ShapeDtypeStruct((copies * sets * quarter, rows), f32),
            jax.ShapeDtypeStruct((clusters, rows), f32),
        ],
        (tile_owner, meta, front_first, damping, *got),
        (SM, SM, SM, VM) + (VM,) * sends,
        (
            pltpu.VMEM((pts_count, send_rows, rows), f32),
            pltpu.VMEM((grp_count, BAND, quarter, rows), f32),
        ),
    )
    ring = layers <= 4

    def along(value):
        if not ring:
            return exchange(value, columns)
        moved = []
        for z in range(1, layers):
            pairs = [(p, (p + GROUP * z) % clusters) for p in range(clusters)]
            moved.append(lax.ppermute(value, AXES, pairs))
        return jnp.concatenate([value, *moved])

    def across(values):
        moved = []
        for i, value in enumerate(values):
            pairs = [(p, p ^ (2 * i + 2)) for p in range(clusters)]
            moved.append(lax.ppermute(value, AXES, pairs))
        return moved

    direct = along(direct)
    direct, mirror, *chunks = lax.optimization_barrier((direct, mirror, *chunks))
    mine = [direct, *across([direct] * 3)]
    theirs = [lax.ppermute(direct, AXES, swap)]
    mirror = along(mirror)
    swapped = lax.ppermute(jnp.concatenate([mirror, chunks[1], chunks[3]]), AXES, swap)
    count = mirror.shape[0]
    chunk = BAND * quarter
    both = jnp.concatenate([mirror, swapped[:count]])
    more = jnp.concatenate([both, chunks[2], swapped[count + chunk :]])
    both, more, *mine = lax.optimization_barrier((both, more, *mine))
    theirs += [lax.ppermute(x, AXES, swap) for x in mine[1:]]
    sides = [mirror, swapped, *across([more, both, both]), chunks[0]]

    width = FRONT * rows
    dims = (pts_count, grp_count, quarter, clusters)
    tall = BEFORE * rows + 8
    tail = (FRONT + BEFORE) * rows + 8 * FRONT
    shapes = (
        ((tail, rows), f32),
        ((width, width), bf16),
        ((width, width), bf16),
        ((tall, width), bf16),
        ((tall, width), bf16),
    )
    stored = call(
        functools.partial(factor_kernel, dims + (ring,)),
        [jax.ShapeDtypeStruct(*x) for x in shapes],
        (meta, front_first, tile_owner, reduced, *mine, *theirs),
        (SM, SM, SM, VM) + (VM,) * GROUP,
        [
            pltpu.VMEM((FRONT, rows, width), f32),
            pltpu.VMEM((tall, width), f32),
            pltpu.VMEM((clusters, sets * quarter, rows), f32),
            pltpu.VMEM((rows + STRIP, 2 * rows), f32),
            pltpu.VMEM((rows, 2 * rows), f32),
            pltpu.VMEM((FRONT, rows, 2 * width), f32),
            pltpu.VMEM((tall, width), f32),
        ],
        flops=400 * rows * rows * rows * 6,
    )
    return tuple(call(
        functools.partial(update_kernel, dims + (ring,)),
        [
            jax.ShapeDtypeStruct((BAND, rows, rows), f32),
            jax.ShapeDtypeStruct((1, rows), f32),
            jax.ShapeDtypeStruct((WINDOW * rows, rows), f32),
        ],
        (meta, front_first, tile_owner, reduced, *sides, *stored),
        (SM, SM, SM, VM) + (VM,) * 11,
        [
            pltpu.VMEM((BEFORE * rows, width), f32),
            pltpu.VMEM((BEFORE * rows, width), bf16),
            pltpu.VMEM((BEFORE * rows, width), bf16),
            pltpu.VMEM((clusters, sets * quarter, rows), f32),
        ],
        flops=200 * rows * rows * rows * 6,
    ))


def solution(mesh):
    in_specs = (
        P(AXES, None, None, None, None),
        P(AXES, None, None),
        P(AXES, None, None),
        P(AXES, None),
        P(),
        P(AXES, None),
        P(),
        P(),
    )
    out_specs = (P(AXES, None, None), P(AXES, None), P(None, "grp"))

    return jax.shard_map(per_device, mesh=mesh, in_specs=in_specs, out_specs=out_specs, check_vma=False)
```

```python
import functools

import jax
import jax.numpy as jnp
from jax import lax
from jax.experimental import pallas as pl
from jax.experimental.pallas import tpu as pltpu
from jax.sharding import PartitionSpec as P


TOUCH = 6
BAND = 8
FRONT = 4
BEFORE = BAND - 1
WINDOW = 2 * BAND - 2 + FRONT
PAIRS = TOUCH * (TOUCH + 1) // 2
GROUP = 8
SPAN = 2 * BAND - 1
STRIP = 8
AXES = ("pts", "grp")
VM = pltpu.VMEM
SM = pltpu.SMEM


def spec(space):
    return pl.BlockSpec(memory_space=space)


def size_of(shape, dtype):
    total = jnp.dtype(dtype).itemsize
    for extent in shape:
        total *= extent
    return total


def call(kernel, out_shapes, args, spaces, scratch=(), flops=0):
    moved = sum(size_of(x.shape, x.dtype) for x, s in zip(args, spaces) if s is VM)
    moved += sum(size_of(x.shape, x.dtype) for x in jax.tree.leaves(out_shapes))
    kept = 0
    for x in scratch:
        if x.memory_space is VM:
            kept += size_of(x.shape, x.dtype)
    limit = min(moved + kept + (8 << 20), 60 << 20)
    return pl.pallas_call(
        kernel,
        out_shape=out_shapes,
        in_specs=[spec(s) for s in spaces],
        out_specs=[spec(VM)] * len(out_shapes),
        scratch_shapes=list(scratch),
        cost_estimate=pl.CostEstimate(flops=flops, bytes_accessed=moved, transcendentals=0),
        compiler_params=pltpu.CompilerParams(vmem_limit_bytes=limit),
    )(*args)


NT = (((1,), (1,)), ((), ()))
TN = (((0,), (0,)), ((), ()))
NN = (((1,), (0,)), ((), ()))


def product(a, b, dims):
    return lax.dot_general(a, b, dims, preferred_element_type=jnp.float32)


def halves(x):
    high = x.astype(jnp.bfloat16)
    return high, (x - high.astype(jnp.float32)).astype(jnp.bfloat16)


def product3(a, b, dims):
    return (
        product(a[0], b[0], dims) + product(a[0], b[1], dims) + product(a[1], b[0], dims)
    )


def pair_index(a, b):
    return (TOUCH - 1) * a - (a * (a - 1)) // 2 + b


def pair_kernel(dims, meta, incidence, jac, blocks, grad, cam, *refs):
    rows, points, piece, grp_count, clusters = dims
    outs, (out, scaled, plain, rhs, pulls) = refs[:GROUP], refs[GROUP:]
    slots = [lax.rem(incidence[0, k] + clusters - meta[2], clusters) for k in range(TOUCH)]
    ranks = [
        sum((slots[m] < slots[k]).astype(jnp.int32) for m in range(TOUCH) if m != k)
        for k in range(TOUCH)
    ]
    v00, v11, v22 = blocks[0:1, :], blocks[1:2, :], blocks[2:3, :]
    v01, v02, v12 = blocks[3:4, :], blocks[4:5, :], blocks[5:6, :]
    a00 = v11 * v22 - v12 * v12
    a11 = v00 * v22 - v02 * v02
    a22 = v00 * v11 - v01 * v01
    a01 = v02 * v12 - v01 * v22
    a02 = v01 * v12 - v11 * v02
    a12 = v01 * v02 - v00 * v12
    inv = 1.0 / (v00 * a00 + v01 * a01 + v02 * a02)
    vinv = [
        [a00 * inv, a01 * inv, a02 * inv],
        [a01 * inv, a11 * inv, a12 * inv],
        [a02 * inv, a12 * inv, a22 * inv],
    ]
    rhs[...] = jnp.zeros_like(rhs)
    rhs[0:1, :] = cam[...]
    wide_grad = grad[...].astype(jnp.float32)
    for c in range(3):
        pulls[:, c * points : (c + 1) * points] = jnp.broadcast_to(
            wide_grad[c : c + 1, :], (16, points)
        ).astype(jnp.bfloat16)
    for a in range(TOUCH):
        k = sum(jnp.where(ranks[m] == a, m, 0) for m in range(TOUCH))
        t = sum(jnp.where(ranks[m] == a, slots[m], 0) for m in range(TOUCH))
        parts = [jac[c, k] for c in range(3)]
        wide = [x.astype(jnp.float32) for x in parts]
        for c in range(3):
            total = wide[0] * vinv[0][c] + wide[1] * vinv[1][c] + wide[2] * vinv[2][c]
            scaled[a, :, c * points : (c + 1) * points] = total.astype(jnp.bfloat16)
            plain[a * rows : (a + 1) * rows, c * points : (c + 1) * points] = parts[c]
        pulled = product(pulls[...], scaled[a], NT)
        rhs[pl.ds(t, 1), :] = rhs[pl.ds(t, 1), :] - pulled[0:1, :]
    for a in range(TOUCH):
        tiles = product(scaled[a], plain[a * rows : TOUCH * rows, :], NT)
        for b in range(a, TOUCH):
            at = pair_index(a, b) * piece
            for e in range(GROUP):
                first = (e % grp_count) * (rows // grp_count) + (e // grp_count) * piece
                out[e, at : at + piece, :] = tiles[
                    first : first + piece, (b - a) * rows : (b - a + 1) * rows
                ]
    lane = lax.broadcasted_iota(jnp.int32, (BAND, rows), 1)
    early = lax.rem(lane // BAND, BAND)
    late = early + lax.rem(lane, BAND)
    ones = jnp.ones_like(lane)
    none = jnp.zeros_like(lane)
    less, less_late, hit, hit_late = none, none, none, none
    for k in range(TOUCH):
        less = less + jnp.where(early > slots[k], ones, none)
        less_late = less_late + jnp.where(late > slots[k], ones, none)
        hit = hit + jnp.where(early == slots[k], ones, none)
        hit_late = hit_late + jnp.where(late == slots[k], ones, none)
    pick = jnp.where(hit * hit_late > 0, pair_index(less, less_late), -1).astype(jnp.float32)
    tail = PAIRS * piece
    for e in range(GROUP):
        out[e, tail : tail + BAND, :] = rhs[...]
        out[e, tail + BAND : tail + 2 * BAND, :] = pick
    place = lax.rem(meta[2], GROUP)
    for bit in range(GROUP):
        outs[bit][...] = out[place ^ bit]


def merge_kernel(dims, owner, meta, *refs):
    piece, pts_count, capacity, sends = dims
    arrived, outs = refs[:GROUP], refs[GROUP : GROUP + sends]
    got, out, rhs, table, pick, sem = refs[GROUP + sends :]
    place = lax.rem(meta[2], GROUP)
    for bit in range(GROUP):
        got[place ^ bit] = arrived[bit][...]
    flip = meta[0] if sends > 1 else 0
    base = lax.rem(meta[2] // GROUP * (GROUP * BAND), pts_count)
    tail = PAIRS * piece
    for j in range(GROUP):
        row = got[j, tail + BAND : tail + 2 * BAND, :]
        table[j : j + 1, :] = row[0:1, :].astype(jnp.int32)
    copy = pltpu.make_async_copy(table, pick, sem)
    copy.start()
    copy.wait()
    for row in range(SPAN):
        for offset in range(BAND):
            if row + offset >= SPAN:
                continue
            total = None
            for j in range(GROUP):
                t = row - j
                if t < 0 or t + offset > BAND - 1:
                    continue
                at = pick[j, t * BAND + offset]
                start = pl.multiple_of(jnp.maximum(at, 0) * piece, piece)
                value = jnp.where(at >= 0, got[j, pl.ds(start, piece), :], 0.0)
                total = value if total is None else total + value
            relative = BAND * row + offset
            dest = owner[lax.rem(base + relative, pts_count)]
            slot = relative // pts_count
            out[dest ^ flip, slot * piece : (slot + 1) * piece, :] = total
    rhs[...] = jnp.zeros_like(rhs)
    for j in range(GROUP):
        rhs[j : j + BAND, :] = rhs[j : j + BAND, :] + got[j, PAIRS * piece : PAIRS * piece + BAND, :]
    share = pl.ds(pl.multiple_of(place // (GROUP // 2) * BAND, BAND), BAND)
    for dest in range(pts_count):
        out[dest, capacity * piece : capacity * piece + BAND, :] = rhs[share, :]
    for bit in range(sends):
        outs[bit][...] = out[bit] if sends > 1 else out[...]


def residue_of(owner, meta, pts_count):
    return sum(jnp.where(owner[i] == meta[0], i, 0) for i in range(pts_count))


def owner_kernel(
    dims, owner, meta, front, damping, *refs
):
    piece, pts_count, capacity, grp_count, quarter, clusters, sets, sends = dims
    arrived = refs[:sends]
    outs = refs[sends : sends + grp_count]
    direct, mirror, reduced, got, rows_out = refs[sends + grp_count :]
    for bit in range(sends):
        if sends > 1:
            got[meta[0] ^ bit] = arrived[bit][...]
        else:
            got[...] = arrived[0][...]
    residue, my_grp, start = residue_of(owner, meta, pts_count), meta[1], front[0]
    members = GROUP // grp_count
    planes = clusters // GROUP
    cols = rows_out.shape[3]
    offset = lax.rem(residue, BAND)
    part = residue // BAND
    stride = pts_count // BAND
    diag = (
        lax.broadcasted_iota(jnp.int32, (quarter, cols), 0) + my_grp * quarter
        == lax.broadcasted_iota(jnp.int32, (quarter, cols), 1)
    )
    diag = diag & (offset == 0)
    for m in range(BAND * grp_count):
        home = (residue + pts_count * m) // BAND
        plane = home // GROUP
        row = lax.rem(home, GROUP)
        before = lax.rem(plane + planes - 1, planes)
        near = (BAND * row + offset) // pts_count
        far = (BAND * (row + GROUP) + offset) // pts_count
        has_far = row + GROUP + offset < SPAN
        far = jnp.where(has_far, far, 0)
        for y in range(members):
            value = got[plane * members + y, pl.ds(pl.multiple_of(near * piece, piece), piece), :]
            extra = got[before * members + y, pl.ds(pl.multiple_of(far * piece, piece), piece), :]
            total = value + jnp.where(has_far, extra, 0.0)
            part_diag = diag[y * piece : (y + 1) * piece, :]
            total = total + jnp.where(part_diag, damping[pl.ds(home, 1), :], 0.0)
            rows_out[(m // BAND) ^ my_grp, m % BAND, y * piece : (y + 1) * piece, :] = total
    for i in range(sets):
        j = lax.rem(part + 2 * clusters - start, stride) + stride * i
        home = lax.rem(start + jnp.minimum(j, FRONT - 1), clusters)
        at = (BAND * home + offset) // pts_count
        value = rows_out[(at // BAND) ^ my_grp, lax.rem(at, BAND)]
        j = lax.rem(part + 2 * clusters - start + offset, stride) + stride * i
        home = lax.rem(start + jnp.minimum(j, FRONT - 1) + clusters - offset, clusters)
        at = (BAND * home + offset) // pts_count
        other = rows_out[(at // BAND) ^ my_grp, lax.rem(at, BAND)]
        for layer in range(direct.shape[0] // (sets * quarter)):
            at = (layer * sets + i) * quarter
            direct[at : at + quarter, :] = value
            mirror[at : at + quarter, :] = other
    for bit in range(grp_count):
        for i in range(BAND):
            outs[bit][i * quarter : (i + 1) * quarter, :] = rows_out[bit, i]
    tail = capacity * piece
    for plane in range(planes):
        before = (plane + planes - 1) % planes
        reduced[plane * GROUP : (plane + 1) * GROUP, :] = (
            got[plane * members, tail : tail + BAND, :]
            + got[before * members + 1, tail : tail + BAND, :]
        )


def gather(gathered, sides, meta, clusters, ring):
    layers = clusters // GROUP
    place, level = lax.rem(meta[2], GROUP), meta[2] // GROUP
    for i in range(GROUP // 2):
        for z in range(layers):
            at = lax.rem(level + layers - z, layers) if ring else z
            at = at * GROUP + (place ^ (2 * i))
            count = gathered.shape[1]
            ref, first = sides[i]
            gathered[at] = ref[first + z * count : first + (z + 1) * count, :]
            ref, first = sides[GROUP // 2 + i]
            gathered[at ^ 1] = ref[first + z * count : first + (z + 1) * count, :]


def fetch(gathered, owner, tile, slot, dims):
    pts_count, grp_count, quarter = dims
    source = owner[lax.rem(tile, pts_count)] * grp_count
    rows = slice(slot * quarter, (slot + 1) * quarter)
    return jnp.concatenate([gathered[source + g, rows, :] for g in range(grp_count)], axis=0)


def factor_kernel(dims, meta, front, owner, reduced, *refs):
    pts_count, grp_count, quarter, clusters, ring = dims
    sides = [(ref, 0) for ref in refs[:GROUP]]
    tail_out, solve_high, solve_low, behind_high, behind_low = refs[GROUP : GROUP + 5]
    upper, behind, gathered, work, done, square, wide = refs[GROUP + 5 :]
    rows = done.shape[0]
    width = FRONT * rows
    start = front[0]
    stride = pts_count // BAND
    after = BAND - 1
    last = after * rows
    gather(gathered, sides, meta, clusters, ring)
    work[rows:, :] = jnp.zeros((STRIP, 2 * rows), jnp.float32)
    wide[...] = jnp.zeros_like(wide)
    upper[...] = jnp.zeros_like(upper)
    square[...] = jnp.zeros_like(square)
    row_id = lax.broadcasted_iota(jnp.int32, (rows, 1), 0)
    col_id = lax.broadcasted_iota(jnp.int32, (1, rows), 1)
    eye = (row_id == col_id).astype(jnp.float32)
    for j in range(FRONT):
        home = lax.rem(start + j, clusters)
        for e in range(BAND):
            tile = fetch(
                gathered, owner, BAND * home + e, j // stride, (pts_count, grp_count, quarter)
            )
            if j + e < FRONT:
                if e == 0:
                    tile = 0.5 * (tile + tile.T)
                square[j, :, (j + e) * rows : (j + e + 1) * rows] = tile
            else:
                at = (j + e - FRONT) * rows
                wide[at : at + rows, j * rows : (j + 1) * rows] = tile.T
        wide[last : last + 1, j * rows : (j + 1) * rows] = reduced[pl.ds(home, 1), :]
    for j in range(FRONT):
        here = j * rows
        work[0:rows, 0:rows] = square[j, :, here : here + rows]
        work[0:rows, rows : 2 * rows] = eye
        eliminate(work, done, rows)
        inverse = jnp.where(row_id >= col_id, done[:, rows : 2 * rows], 0.0)
        pair = halves(inverse)
        upper[j, :, here : here + rows] = jnp.where(row_id <= col_id, done[:, 0:rows], 0.0)
        parts = []
        if j < FRONT - 1:
            parts.append(square[j, :, here + rows : width])
        if j > 0:
            parts.append(square[j, :, width : width + here])
        line = product3(pair, halves(jnp.concatenate(parts, axis=1)), NN)
        ahead = width - here - rows
        if ahead:
            upper[j, :, here + rows :] = line[:, 0:ahead]
        solve = jnp.concatenate([line[:, ahead:], inverse], axis=1) if j else inverse
        high, low = halves(solve)
        solve_high[here : here + rows, 0 : here + rows] = high
        solve_low[here : here + rows, 0 : here + rows] = low
        if j < FRONT - 1:
            zero = jnp.zeros((rows, ahead), jnp.bfloat16)
            solve_high[here : here + rows, here + rows :] = zero
            solve_low[here : here + rows, here + rows :] = zero
            both = halves(line[:, 0:ahead])
            for i in range(j + 1, FRONT):
                skip = (i - j - 1) * rows
                left = tuple(x[:, skip : skip + rows] for x in both)
                right = tuple(
                    jnp.concatenate([x[:, skip:], y], axis=1) for x, y in zip(both, (high, low))
                )
                change = product3(left, right, TN)
                cut = width - i * rows
                square[i, :, i * rows : width] = square[i, :, i * rows : width] - change[:, 0:cut]
                square[i, :, width : width + here + rows] = (
                    square[i, :, width : width + here + rows] - change[:, cut:]
                )
    result = solve_rows(wide, solve_high, solve_low)
    high, low = halves(result)
    behind_high[...] = high
    behind_low[...] = low
    behind[...] = result
    first = pl.ds(pl.multiple_of(meta[1] * rows, rows), rows)
    for j in range(FRONT):
        tail_out[j * rows : (j + 1) * rows, :] = upper[meta[1], :, j * rows : (j + 1) * rows].T
    tail_out[FRONT * rows : FRONT * rows + last, :] = behind[0:last, first]
    for j in range(FRONT):
        at = FRONT * rows + last + 8 * j
        tail_out[at : at + 8, :] = result[last : last + 8, j * rows : (j + 1) * rows]


def eliminate(work, done, rows):
    lanes = lax.broadcasted_iota(jnp.int32, (STRIP, rows), 1)
    subs = lax.broadcasted_iota(jnp.int32, (STRIP, rows), 0)

    def strip(p, carry):
        now, past = carry
        at = pl.multiple_of(p * STRIP, STRIP)
        lhs = jnp.where(lanes >= at + STRIP, past[:, 0:rows], 0.0)
        work[0:rows, :] = work[0:rows, :] - product3(halves(lhs), halves(past), TN)
        now_a, now_i = now[:, 0:rows], now[:, rows : 2 * rows]
        shift = lax.rem(rows - at, rows)
        turned = pltpu.roll(now_a, shift, 1)
        turned_next = turned.T[STRIP : 2 * STRIP, :]
        column = [jnp.broadcast_to(turned[:, i : i + 1], (STRIP, rows)) for i in range(STRIP)]
        below = [jnp.broadcast_to(turned_next[:, i : i + 1], (STRIP, rows)) for i in range(STRIP)]
        norm = jnp.zeros((STRIP, rows), jnp.float32)
        next_a, next_i = norm, norm

        def row(value, i):
            return jnp.broadcast_to(value[i : i + 1, :], (STRIP, rows))

        for i in range(0, STRIP, 2):
            a, b, c = row(column[i], i), row(column[i + 1], i), row(column[i + 1], i + 1)
            det = a * c - b * b
            inv = 1.0 / a
            inv_second = a * (1.0 / det)
            ratio = b * inv
            norm = jnp.where(subs == i, lax.rsqrt(a), norm)
            norm = jnp.where(subs == i + 1, lax.rsqrt(det * inv), norm)
            scale = jnp.where(subs > i, column[i] * inv, 0.0)
            scale_next = below[i] * inv
            second = jnp.where(subs > i + 1, (column[i + 1] - scale * b) * inv_second, 0.0)
            second_next = (below[i + 1] - scale_next * b) * inv_second
            for k in range(i + 2, STRIP):
                top = row(column[k], i)
                low = row(column[k], i + 1) - ratio * top
                column[k] = column[k] - scale * top - second * low
                below[k] = below[k] - scale_next * top - second_next * low
            line_a, line_i = row(now_a, i), row(now_i, i)
            low_a = row(now_a, i + 1) - ratio * line_a
            low_i = row(now_i, i + 1) - ratio * line_i
            now_a = now_a - scale * line_a - second * low_a
            now_i = now_i - scale * line_i - second * low_i
            next_a = next_a + (scale_next * line_a + second_next * low_a)
            next_i = next_i + (scale_next * line_i + second_next * low_i)
        finished = jnp.concatenate([now_a * norm, now_i * norm], axis=1)
        done[pl.ds(at, STRIP), :] = finished
        ahead = work[pl.ds(at + STRIP, STRIP), :]
        return (ahead - jnp.concatenate([next_a, next_i], axis=1), finished)

    first = work[0:STRIP, :]
    lax.fori_loop(0, rows // STRIP, strip, (first, jnp.zeros_like(first)))


def solve_rows(wide, solve_high, solve_low):
    half = solve_high.shape[0] // 2
    high, low = halves(wide[...])
    left = product3(
        (high[:, :half], low[:, :half]),
        (solve_high[:half, :half], solve_low[:half, :half]),
        NT,
    )
    right = product3((high, low), (solve_high[half:, :], solve_low[half:, :]), NT)
    return jnp.concatenate([left, right], axis=1)


def update_kernel(dims, meta, front, owner, reduced, *refs):
    pts_count, grp_count, quarter, clusters, ring = dims
    first, swapped, second, third, fourth, kept_chunk = refs[:6]
    refs = refs[6:]
    count = first.shape[0]
    chunk = BAND * quarter
    crossed = (second, third, fourth)
    sides = [(first, 0)] + [(ref, 0) for ref in crossed]
    sides += [(swapped, 0)] + [(ref, count) for ref in crossed]
    chunks = (
        (kept_chunk, 0), (swapped, count), (second, 2 * count), (second, 2 * count + chunk)
    )
    tail, solve_high, solve_low, behind_high, behind_low = refs[:5]
    tiles_out, rhs_out, panel_out, wide, ahead_high, ahead_low, gathered = refs[5:]
    rows = tiles_out.shape[1]
    residue, my_grp, start = residue_of(owner, meta, pts_count), meta[1], front[0]
    device = meta[2]
    stride = pts_count // BAND
    gather(gathered, sides, meta, clusters, ring)
    wide[...] = jnp.zeros_like(wide)
    for j in range(FRONT):
        for i in range(j, BEFORE):
            e = BEFORE + j - i
            home = lax.rem(start + j + clusters - e, clusters)
            tile = fetch(
                gathered, owner, BAND * home + e, j // stride, (pts_count, grp_count, quarter)
            )
            wide[i * rows : (i + 1) * rows, j * rows : (j + 1) * rows] = tile
    result = solve_rows(wide, solve_high, solve_low)
    wide[...] = result
    high, low = halves(result)
    ahead_high[...] = high
    ahead_low[...] = low
    first = pl.ds(pl.multiple_of(my_grp * rows, rows), rows)
    panel_out[0 : BEFORE * rows, :] = wide[:, first]
    panel_out[BEFORE * rows :, :] = tail[0 : (BEFORE + FRONT) * rows, :]
    base = start + clusters - BEFORE

    def ahead(position):
        at = pl.ds(pl.multiple_of(position * rows, rows), rows)
        return (ahead_high[at, :], ahead_low[at, :])

    def past(position):
        at = pl.ds(pl.multiple_of((position - BEFORE - FRONT) * rows, rows), rows)
        return (behind_high[at, :], behind_low[at, :])

    def is_ahead(position):
        return position < BEFORE

    def is_past(position):
        return (position < WINDOW) & (position >= BEFORE + FRONT)

    for i in range(BAND):
        tile = residue + pts_count * (BAND * my_grp + i)
        home = tile // BAND
        offset = lax.rem(tile, BAND)
        one = lax.rem(home + 2 * clusters - base, clusters)
        two = lax.rem(home + offset + 2 * clusters - base, clusters)
        for bit in range(grp_count):
            at = pl.multiple_of((my_grp ^ bit) * quarter, quarter)
            ref, begin = chunks[bit]
            begin = begin + i * quarter
            tiles_out[i, pl.ds(at, quarter), :] = ref[begin : begin + quarter, :]
        for left, right, test_left, test_right in (
            (ahead, ahead, is_ahead, is_ahead),
            (ahead, past, is_ahead, is_past),
            (past, past, is_past, is_past),
        ):
            @pl.when(test_left(one) & test_right(two))
            def _():
                tiles_out[i] = tiles_out[i] - product3(left(one), right(two), NT)

    position = lax.rem(device + 2 * clusters - base, clusters)
    mine = reduced[pl.ds(device, 1), :]
    rhs_out[...] = mine
    last = (BEFORE + FRONT) * rows
    front_row = [tail[last + 8 * j : last + 8 * j + 8, :] for j in range(FRONT)]
    for take, test in ((ahead, is_ahead), (past, is_past)):
        @pl.when(test(position))
        def _():
            known = halves(jnp.concatenate(front_row, axis=1))
            rhs_out[...] = mine - product3(known, take(position), NT)[0:1, :]

    @pl.when((position >= BEFORE) & (position < BEFORE + FRONT))
    def _():
        at = pl.multiple_of(last + 8 * (position - BEFORE), 8)
        rhs_out[...] = tail[pl.ds(at, 8), :][0:1, :]


def per_device(
    jacobian, point_blocks, point_grad, camera_grad, damping, incidence, tile_owner, front_first
):
    pts_count = lax.axis_size("pts")
    grp_count = lax.axis_size("grp")
    clusters = pts_count * grp_count
    my_grp = lax.axis_index("grp")
    my_pts = lax.axis_index("pts")
    device = my_pts * grp_count + my_grp
    rows = jacobian.shape[2]
    points = jacobian.shape[4]
    piece = rows // GROUP
    quarter = rows // grp_count
    capacity = (BAND * (SPAN - 1)) // pts_count + 1
    stride = pts_count // BAND
    sets = -(-FRONT // stride)
    f32 = jnp.float32
    layers = clusters // GROUP
    columns = [[GROUP * z + e for z in range(layers)] for e in range(GROUP)]
    swap = [(i, i ^ 1) for i in range(clusters)]

    def flip(values, axis, count):
        moved = [
            lax.ppermute(value, axis, [(p, p ^ (bit + 1)) for p in range(count)])
            for bit, value in enumerate(values[1:])
        ]
        return [values[0], *moved]

    def exchange(value, lists):
        return lax.all_to_all(
            value, AXES, split_axis=0, concat_axis=0, tiled=True, axis_index_groups=lists
        )

    lane = jnp.arange(8)
    meta = jnp.where(lane == 0, my_pts, jnp.where(lane == 1, my_grp, device)).astype(jnp.int32)
    bf16 = jnp.bfloat16
    jac = jnp.transpose(jacobian[0], (2, 0, 1, 3))
    block_rows = PAIRS * piece + 2 * BAND
    sent = call(
        functools.partial(pair_kernel, (rows, points, piece, grp_count, clusters)),
        [jax.ShapeDtypeStruct((block_rows, rows), f32)] * GROUP,
        (meta, incidence, jac, point_blocks[0], point_grad[0], camera_grad),
        (SM, SM, VM, VM, VM, VM),
        (
            pltpu.VMEM((GROUP, block_rows, rows), f32),
            pltpu.VMEM((TOUCH, rows, 3 * points), bf16),
            pltpu.VMEM((TOUCH * rows, 3 * points), bf16),
            pltpu.VMEM((BAND, rows), f32),
            pltpu.VMEM((16, 3 * points), bf16),
        ),
        flops=2 * PAIRS * rows * rows * 3 * points,
    )
    got = flip(sent, AXES, clusters)
    sends = pts_count if pts_count <= GROUP else 1
    send_rows = capacity * piece + BAND
    shape = (send_rows, rows) if sends > 1 else (pts_count, send_rows, rows)
    sent = call(
        functools.partial(merge_kernel, (piece, pts_count, capacity, sends)),
        [jax.ShapeDtypeStruct(shape, f32)] * sends,
        (tile_owner, meta, *got),
        (SM, SM) + (VM,) * GROUP,
        (
            pltpu.VMEM((GROUP, block_rows, rows), f32),
            pltpu.VMEM((pts_count, send_rows, rows), f32),
            pltpu.VMEM((2 * BAND, rows), f32),
            pltpu.VMEM((GROUP, rows), jnp.int32),
            pltpu.SMEM((GROUP, rows), jnp.int32),
            pltpu.SemaphoreType.DMA(()),
        ),
    )
    if sends > 1:
        got = flip(sent, "pts", pts_count)
    else:
        got = [lax.all_to_all(sent[0], "pts", split_axis=0, concat_axis=0, tiled=True)]
    copies = layers if layers > 4 else 1
    *chunks, direct, mirror, reduced = call(
        functools.partial(
            owner_kernel,
            (piece, pts_count, capacity, grp_count, quarter, clusters, sets, sends),
        ),
        [jax.ShapeDtypeStruct((BAND * quarter, rows), f32)] * grp_count
        + [
            jax.ShapeDtypeStruct((copies * sets * quarter, rows), f32),
            jax.ShapeDtypeStruct((copies * sets * quarter, rows), f32),
            jax.ShapeDtypeStruct((clusters, rows), f32),
        ],
        (tile_owner, meta, front_first, damping, *got),
        (SM, SM, SM, VM) + (VM,) * sends,
        (
            pltpu.VMEM((pts_count, send_rows, rows), f32),
            pltpu.VMEM((grp_count, BAND, quarter, rows), f32),
        ),
    )
    ring = layers <= 4

    def along(value):
        if not ring:
            return exchange(value, columns)
        moved = []
        for z in range(1, layers):
            pairs = [(p, (p + GROUP * z) % clusters) for p in range(clusters)]
            moved.append(lax.ppermute(value, AXES, pairs))
        return jnp.concatenate([value, *moved])

    def across(values):
        moved = []
        for i, value in enumerate(values):
            pairs = [(p, p ^ (2 * i + 2)) for p in range(clusters)]
            moved.append(lax.ppermute(value, AXES, pairs))
        return moved

    direct = along(direct)
    direct, mirror, *chunks = lax.optimization_barrier((direct, mirror, *chunks))
    mine = [direct, *across([direct] * 3)]
    theirs = [lax.ppermute(direct, AXES, swap)]
    mirror = along(mirror)
    swapped = lax.ppermute(jnp.concatenate([mirror, chunks[1], chunks[3]]), AXES, swap)
    count = mirror.shape[0]
    chunk = BAND * quarter
    both = jnp.concatenate([mirror, swapped[:count]])
    more = jnp.concatenate([both, chunks[2], swapped[count + chunk :]])
    both, more, mine[-1] = lax.optimization_barrier((both, more, mine[-1]))
    theirs += [lax.ppermute(x, AXES, swap) for x in mine[1:]]
    sides = [mirror, swapped, *across([more, both, both]), chunks[0]]

    width = FRONT * rows
    dims = (pts_count, grp_count, quarter, clusters)
    tall = BEFORE * rows + 8
    tail = (FRONT + BEFORE) * rows + 8 * FRONT
    shapes = (
        ((tail, rows), f32),
        ((width, width), bf16),
        ((width, width), bf16),
        ((tall, width), bf16),
        ((tall, width), bf16),
    )
    stored = call(
        functools.partial(factor_kernel, dims + (ring,)),
        [jax.ShapeDtypeStruct(*x) for x in shapes],
        (meta, front_first, tile_owner, reduced, *mine, *theirs),
        (SM, SM, SM, VM) + (VM,) * GROUP,
        [
            pltpu.VMEM((FRONT, rows, width), f32),
            pltpu.VMEM((tall, width), f32),
            pltpu.VMEM((clusters, sets * quarter, rows), f32),
            pltpu.VMEM((rows + STRIP, 2 * rows), f32),
            pltpu.VMEM((rows, 2 * rows), f32),
            pltpu.VMEM((FRONT, rows, 2 * width), f32),
            pltpu.VMEM((tall, width), f32),
        ],
        flops=400 * rows * rows * rows * 6,
    )
    return tuple(call(
        functools.partial(update_kernel, dims + (ring,)),
        [
            jax.ShapeDtypeStruct((BAND, rows, rows), f32),
            jax.ShapeDtypeStruct((1, rows), f32),
            jax.ShapeDtypeStruct((WINDOW * rows, rows), f32),
        ],
        (meta, front_first, tile_owner, reduced, *sides, *stored),
        (SM, SM, SM, VM) + (VM,) * 11,
        [
            pltpu.VMEM((BEFORE * rows, width), f32),
            pltpu.VMEM((BEFORE * rows, width), bf16),
            pltpu.VMEM((BEFORE * rows, width), bf16),
            pltpu.VMEM((clusters, sets * quarter, rows), f32),
        ],
        flops=200 * rows * rows * rows * 6,
    ))


def solution(mesh):
    in_specs = (
        P(AXES, None, None, None, None),
        P(AXES, None, None),
        P(AXES, None, None),
        P(AXES, None),
        P(),
        P(AXES, None),
        P(),
        P(),
    )
    out_specs = (P(AXES, None, None), P(AXES, None), P(None, "grp"))

    return jax.shard_map(per_device, mesh=mesh, in_specs=in_specs, out_specs=out_specs, check_vma=False)
```

```python
import functools

import jax
import jax.numpy as jnp
from jax import lax
from jax.experimental import pallas as pl
from jax.experimental.pallas import tpu as pltpu
from jax.sharding import PartitionSpec as P


TOUCH = 6
BAND = 8
FRONT = 4
BEFORE = BAND - 1
WINDOW = 2 * BAND - 2 + FRONT
PAIRS = TOUCH * (TOUCH + 1) // 2
GROUP = 8
SPAN = 2 * BAND - 1
STRIP = 8
AXES = ("pts", "grp")
VM = pltpu.VMEM
SM = pltpu.SMEM


def spec(space):
    return pl.BlockSpec(memory_space=space)


def size_of(shape, dtype):
    total = jnp.dtype(dtype).itemsize
    for extent in shape:
        total *= extent
    return total


def call(kernel, out_shapes, args, spaces, scratch=(), flops=0):
    moved = sum(size_of(x.shape, x.dtype) for x, s in zip(args, spaces) if s is VM)
    moved += sum(size_of(x.shape, x.dtype) for x in jax.tree.leaves(out_shapes))
    kept = 0
    for x in scratch:
        if x.memory_space is VM:
            kept += size_of(x.shape, x.dtype)
    limit = min(moved + kept + (8 << 20), 60 << 20)
    return pl.pallas_call(
        kernel,
        out_shape=out_shapes,
        in_specs=[spec(s) for s in spaces],
        out_specs=[spec(VM)] * len(out_shapes),
        scratch_shapes=list(scratch),
        cost_estimate=pl.CostEstimate(flops=flops, bytes_accessed=moved, transcendentals=0),
        compiler_params=pltpu.CompilerParams(vmem_limit_bytes=limit),
    )(*args)


NT = (((1,), (1,)), ((), ()))
TN = (((0,), (0,)), ((), ()))
NN = (((1,), (0,)), ((), ()))


def product(a, b, dims):
    return lax.dot_general(a, b, dims, preferred_element_type=jnp.float32)


def halves(x):
    high = x.astype(jnp.bfloat16)
    return high, (x - high.astype(jnp.float32)).astype(jnp.bfloat16)


def product3(a, b, dims):
    return (
        product(a[0], b[0], dims) + product(a[0], b[1], dims) + product(a[1], b[0], dims)
    )


def pair_index(a, b):
    return (TOUCH - 1) * a - (a * (a - 1)) // 2 + b


def pair_kernel(dims, meta, incidence, jac, blocks, grad, cam, *refs):
    rows, points, piece, grp_count, clusters = dims
    outs, (out, scaled, plain, rhs, pulls) = refs[:GROUP], refs[GROUP:]
    slots = [lax.rem(incidence[0, k] + clusters - meta[2], clusters) for k in range(TOUCH)]
    ranks = [
        sum((slots[m] < slots[k]).astype(jnp.int32) for m in range(TOUCH) if m != k)
        for k in range(TOUCH)
    ]
    v00, v11, v22 = blocks[0:1, :], blocks[1:2, :], blocks[2:3, :]
    v01, v02, v12 = blocks[3:4, :], blocks[4:5, :], blocks[5:6, :]
    a00 = v11 * v22 - v12 * v12
    a11 = v00 * v22 - v02 * v02
    a22 = v00 * v11 - v01 * v01
    a01 = v02 * v12 - v01 * v22
    a02 = v01 * v12 - v11 * v02
    a12 = v01 * v02 - v00 * v12
    inv = 1.0 / (v00 * a00 + v01 * a01 + v02 * a02)
    vinv = [
        [a00 * inv, a01 * inv, a02 * inv],
        [a01 * inv, a11 * inv, a12 * inv],
        [a02 * inv, a12 * inv, a22 * inv],
    ]
    rhs[...] = jnp.zeros_like(rhs)
    rhs[0:1, :] = cam[...]
    wide_grad = grad[...].astype(jnp.float32)
    for c in range(3):
        pulls[:, c * points : (c + 1) * points] = jnp.broadcast_to(
            wide_grad[c : c + 1, :], (16, points)
        ).astype(jnp.bfloat16)
    for a in range(TOUCH):
        k = sum(jnp.where(ranks[m] == a, m, 0) for m in range(TOUCH))
        t = sum(jnp.where(ranks[m] == a, slots[m], 0) for m in range(TOUCH))
        parts = [jac[c, k] for c in range(3)]
        wide = [x.astype(jnp.float32) for x in parts]
        for c in range(3):
            total = wide[0] * vinv[0][c] + wide[1] * vinv[1][c] + wide[2] * vinv[2][c]
            scaled[a, :, c * points : (c + 1) * points] = total.astype(jnp.bfloat16)
            plain[a * rows : (a + 1) * rows, c * points : (c + 1) * points] = parts[c]
        pulled = product(pulls[...], scaled[a], NT)
        rhs[pl.ds(t, 1), :] = rhs[pl.ds(t, 1), :] - pulled[0:1, :]
    for a in range(TOUCH):
        tiles = product(scaled[a], plain[a * rows : TOUCH * rows, :], NT)
        for b in range(a, TOUCH):
            at = pair_index(a, b) * piece
            for e in range(GROUP):
                first = (e % grp_count) * (rows // grp_count) + (e // grp_count) * piece
                out[e, at : at + piece, :] = tiles[
                    first : first + piece, (b - a) * rows : (b - a + 1) * rows
                ]
    lane = lax.broadcasted_iota(jnp.int32, (BAND, rows), 1)
    early = lax.rem(lane // BAND, BAND)
    late = early + lax.rem(lane, BAND)
    ones = jnp.ones_like(lane)
    none = jnp.zeros_like(lane)
    less, less_late, hit, hit_late = none, none, none, none
    for k in range(TOUCH):
        less = less + jnp.where(early > slots[k], ones, none)
        less_late = less_late + jnp.where(late > slots[k], ones, none)
        hit = hit + jnp.where(early == slots[k], ones, none)
        hit_late = hit_late + jnp.where(late == slots[k], ones, none)
    pick = jnp.where(hit * hit_late > 0, pair_index(less, less_late), -1).astype(jnp.float32)
    tail = PAIRS * piece
    for e in range(GROUP):
        out[e, tail : tail + BAND, :] = rhs[...]
        out[e, tail + BAND : tail + 2 * BAND, :] = pick
    place = lax.rem(meta[2], GROUP)
    for bit in range(GROUP):
        outs[bit][...] = out[place ^ bit]


def merge_kernel(dims, owner, meta, *refs):
    piece, pts_count, capacity, sends = dims
    arrived, outs = refs[:GROUP], refs[GROUP : GROUP + sends]
    got, out, rhs, table, pick, sem = refs[GROUP + sends :]
    place = lax.rem(meta[2], GROUP)
    for bit in range(GROUP):
        got[place ^ bit] = arrived[bit][...]
    flip = meta[0] if sends > 1 else 0
    base = lax.rem(meta[2] // GROUP * (GROUP * BAND), pts_count)
    tail = PAIRS * piece
    for j in range(GROUP):
        row = got[j, tail + BAND : tail + 2 * BAND, :]
        table[j : j + 1, :] = row[0:1, :].astype(jnp.int32)
    copy = pltpu.make_async_copy(table, pick, sem)
    copy.start()
    copy.wait()
    for row in range(SPAN):
        for offset in range(BAND):
            if row + offset >= SPAN:
                continue
            total = None
            for j in range(GROUP):
                t = row - j
                if t < 0 or t + offset > BAND - 1:
                    continue
                at = pick[j, t * BAND + offset]
                start = pl.multiple_of(jnp.maximum(at, 0) * piece, piece)
                value = jnp.where(at >= 0, got[j, pl.ds(start, piece), :], 0.0)
                total = value if total is None else total + value
            relative = BAND * row + offset
            dest = owner[lax.rem(base + relative, pts_count)]
            slot = relative // pts_count
            out[dest ^ flip, slot * piece : (slot + 1) * piece, :] = total
    rhs[...] = jnp.zeros_like(rhs)
    for j in range(GROUP):
        rhs[j : j + BAND, :] = rhs[j : j + BAND, :] + got[j, PAIRS * piece : PAIRS * piece + BAND, :]
    share = pl.ds(pl.multiple_of(place // (GROUP // 2) * BAND, BAND), BAND)
    for dest in range(pts_count):
        out[dest, capacity * piece : capacity * piece + BAND, :] = rhs[share, :]
    for bit in range(sends):
        outs[bit][...] = out[bit] if sends > 1 else out[...]


def residue_of(owner, meta, pts_count):
    return sum(jnp.where(owner[i] == meta[0], i, 0) for i in range(pts_count))


def owner_kernel(
    dims, owner, meta, front, damping, *refs
):
    piece, pts_count, capacity, grp_count, quarter, clusters, sets, sends = dims
    arrived = refs[:sends]
    outs = refs[sends : sends + grp_count]
    direct, mirror, reduced, got, rows_out = refs[sends + grp_count :]
    for bit in range(sends):
        if sends > 1:
            got[meta[0] ^ bit] = arrived[bit][...]
        else:
            got[...] = arrived[0][...]
    residue, my_grp, start = residue_of(owner, meta, pts_count), meta[1], front[0]
    members = GROUP // grp_count
    planes = clusters // GROUP
    cols = rows_out.shape[3]
    offset = lax.rem(residue, BAND)
    part = residue // BAND
    stride = pts_count // BAND
    diag = (
        lax.broadcasted_iota(jnp.int32, (quarter, cols), 0) + my_grp * quarter
        == lax.broadcasted_iota(jnp.int32, (quarter, cols), 1)
    )
    diag = diag & (offset == 0)
    for m in range(BAND * grp_count):
        home = (residue + pts_count * m) // BAND
        plane = home // GROUP
        row = lax.rem(home, GROUP)
        before = lax.rem(plane + planes - 1, planes)
        near = (BAND * row + offset) // pts_count
        far = (BAND * (row + GROUP) + offset) // pts_count
        has_far = row + GROUP + offset < SPAN
        far = jnp.where(has_far, far, 0)
        for y in range(members):
            value = got[plane * members + y, pl.ds(pl.multiple_of(near * piece, piece), piece), :]
            extra = got[before * members + y, pl.ds(pl.multiple_of(far * piece, piece), piece), :]
            total = value + jnp.where(has_far, extra, 0.0)
            part_diag = diag[y * piece : (y + 1) * piece, :]
            total = total + jnp.where(part_diag, damping[pl.ds(home, 1), :], 0.0)
            rows_out[(m // BAND) ^ my_grp, m % BAND, y * piece : (y + 1) * piece, :] = total
    for i in range(sets):
        j = lax.rem(part + 2 * clusters - start, stride) + stride * i
        home = lax.rem(start + jnp.minimum(j, FRONT - 1), clusters)
        at = (BAND * home + offset) // pts_count
        value = rows_out[(at // BAND) ^ my_grp, lax.rem(at, BAND)]
        j = lax.rem(part + 2 * clusters - start + offset, stride) + stride * i
        home = lax.rem(start + jnp.minimum(j, FRONT - 1) + clusters - offset, clusters)
        at = (BAND * home + offset) // pts_count
        other = rows_out[(at // BAND) ^ my_grp, lax.rem(at, BAND)]
        for layer in range(direct.shape[0] // (sets * quarter)):
            at = (layer * sets + i) * quarter
            direct[at : at + quarter, :] = value
            mirror[at : at + quarter, :] = other
    for bit in range(grp_count):
        for i in range(BAND):
            outs[bit][i * quarter : (i + 1) * quarter, :] = rows_out[bit, i]
    tail = capacity * piece
    for plane in range(planes):
        before = (plane + planes - 1) % planes
        reduced[plane * GROUP : (plane + 1) * GROUP, :] = (
            got[plane * members, tail : tail + BAND, :]
            + got[before * members + 1, tail : tail + BAND, :]
        )


def gather(gathered, sides, meta, clusters, ring):
    layers = clusters // GROUP
    place, level = lax.rem(meta[2], GROUP), meta[2] // GROUP
    for i in range(GROUP // 2):
        for z in range(layers):
            at = lax.rem(level + layers - z, layers) if ring else z
            at = at * GROUP + (place ^ (2 * i))
            count = gathered.shape[1]
            ref, first = sides[i]
            gathered[at] = ref[first + z * count : first + (z + 1) * count, :]
            ref, first = sides[GROUP // 2 + i]
            gathered[at ^ 1] = ref[first + z * count : first + (z + 1) * count, :]


def fetch(gathered, owner, tile, slot, dims):
    pts_count, grp_count, quarter = dims
    source = owner[lax.rem(tile, pts_count)] * grp_count
    rows = slice(slot * quarter, (slot + 1) * quarter)
    return jnp.concatenate([gathered[source + g, rows, :] for g in range(grp_count)], axis=0)


def factor_kernel(dims, meta, front, owner, reduced, *refs):
    pts_count, grp_count, quarter, clusters, ring = dims
    sides = [(ref, 0) for ref in refs[:GROUP]]
    tail_out, solve_high, solve_low, behind_high, behind_low = refs[GROUP : GROUP + 5]
    upper, behind, gathered, work, done, square, wide = refs[GROUP + 5 :]
    rows = done.shape[0]
    width = FRONT * rows
    start = front[0]
    stride = pts_count // BAND
    after = BAND - 1
    last = after * rows
    gather(gathered, sides, meta, clusters, ring)
    work[rows:, :] = jnp.zeros((STRIP, 2 * rows), jnp.float32)
    wide[...] = jnp.zeros_like(wide)
    upper[...] = jnp.zeros_like(upper)
    for j in range(1, FRONT):
        square[j, :, width : width + j * rows] = jnp.zeros((rows, j * rows), jnp.float32)
    row_id = lax.broadcasted_iota(jnp.int32, (rows, 1), 0)
    col_id = lax.broadcasted_iota(jnp.int32, (1, rows), 1)
    eye = (row_id == col_id).astype(jnp.float32)
    for j in range(FRONT):
        home = lax.rem(start + j, clusters)
        for e in range(BAND):
            tile = fetch(
                gathered, owner, BAND * home + e, j // stride, (pts_count, grp_count, quarter)
            )
            if j + e < FRONT:
                if e == 0:
                    tile = 0.5 * (tile + tile.T)
                square[j, :, (j + e) * rows : (j + e + 1) * rows] = tile
            else:
                at = (j + e - FRONT) * rows
                wide[at : at + rows, j * rows : (j + 1) * rows] = tile.T
        wide[last : last + 1, j * rows : (j + 1) * rows] = reduced[pl.ds(home, 1), :]
    for j in range(FRONT):
        here = j * rows
        work[0:rows, 0:rows] = square[j, :, here : here + rows]
        work[0:rows, rows : 2 * rows] = eye
        eliminate(work, done, rows)
        inverse = jnp.where(row_id >= col_id, done[:, rows : 2 * rows], 0.0)
        pair = halves(inverse)
        upper[j, :, here : here + rows] = jnp.where(row_id <= col_id, done[:, 0:rows], 0.0)
        parts = []
        if j < FRONT - 1:
            parts.append(square[j, :, here + rows : width])
        if j > 0:
            parts.append(square[j, :, width : width + here])
        line = product3(pair, halves(jnp.concatenate(parts, axis=1)), NN)
        ahead = width - here - rows
        if ahead:
            upper[j, :, here + rows :] = line[:, 0:ahead]
        solve = jnp.concatenate([line[:, ahead:], inverse], axis=1) if j else inverse
        high, low = halves(solve)
        solve_high[here : here + rows, 0 : here + rows] = high
        solve_low[here : here + rows, 0 : here + rows] = low
        if j < FRONT - 1:
            zero = jnp.zeros((rows, ahead), jnp.bfloat16)
            solve_high[here : here + rows, here + rows :] = zero
            solve_low[here : here + rows, here + rows :] = zero
            both = halves(line[:, 0:ahead])
            for i in range(j + 1, FRONT):
                skip = (i - j - 1) * rows
                left = tuple(x[:, skip : skip + rows] for x in both)
                right = tuple(
                    jnp.concatenate([x[:, skip:], y], axis=1) for x, y in zip(both, (high, low))
                )
                change = product3(left, right, TN)
                cut = width - i * rows
                square[i, :, i * rows : width] = square[i, :, i * rows : width] - change[:, 0:cut]
                square[i, :, width : width + here + rows] = (
                    square[i, :, width : width + here + rows] - change[:, cut:]
                )
    result = solve_rows(wide, solve_high, solve_low)
    high, low = halves(result)
    behind_high[...] = high
    behind_low[...] = low
    behind[...] = result
    first = pl.ds(pl.multiple_of(meta[1] * rows, rows), rows)
    for j in range(FRONT):
        tail_out[j * rows : (j + 1) * rows, :] = upper[meta[1], :, j * rows : (j + 1) * rows].T
    tail_out[FRONT * rows : FRONT * rows + last, :] = behind[0:last, first]
    for j in range(FRONT):
        at = FRONT * rows + last + 8 * j
        tail_out[at : at + 8, :] = result[last : last + 8, j * rows : (j + 1) * rows]


def eliminate(work, done, rows):
    lanes = lax.broadcasted_iota(jnp.int32, (STRIP, rows), 1)
    subs = lax.broadcasted_iota(jnp.int32, (STRIP, rows), 0)

    def strip(p, carry):
        now, past = carry
        at = pl.multiple_of(p * STRIP, STRIP)
        lhs = jnp.where(lanes >= at + STRIP, past[:, 0:rows], 0.0)
        work[0:rows, :] = work[0:rows, :] - product3(halves(lhs), halves(past), TN)
        now_a, now_i = now[:, 0:rows], now[:, rows : 2 * rows]
        shift = lax.rem(rows - at, rows)
        turned = pltpu.roll(now_a, shift, 1)
        turned_next = turned.T[STRIP : 2 * STRIP, :]
        column = [jnp.broadcast_to(turned[:, i : i + 1], (STRIP, rows)) for i in range(STRIP)]
        below = [jnp.broadcast_to(turned_next[:, i : i + 1], (STRIP, rows)) for i in range(STRIP)]
        norm = jnp.zeros((STRIP, rows), jnp.float32)
        next_a, next_i = norm, norm

        def row(value, i):
            return jnp.broadcast_to(value[i : i + 1, :], (STRIP, rows))

        for i in range(0, STRIP, 2):
            a, b, c = row(column[i], i), row(column[i + 1], i), row(column[i + 1], i + 1)
            det = a * c - b * b
            inv = 1.0 / a
            inv_second = a * (1.0 / det)
            ratio = b * inv
            norm = jnp.where(subs == i, lax.rsqrt(a), norm)
            norm = jnp.where(subs == i + 1, lax.rsqrt(det * inv), norm)
            scale = jnp.where(subs > i, column[i] * inv, 0.0)
            scale_next = below[i] * inv
            second = jnp.where(subs > i + 1, (column[i + 1] - scale * b) * inv_second, 0.0)
            second_next = (below[i + 1] - scale_next * b) * inv_second
            for k in range(i + 2, STRIP):
                top = row(column[k], i)
                low = row(column[k], i + 1) - ratio * top
                column[k] = column[k] - scale * top - second * low
                below[k] = below[k] - scale_next * top - second_next * low
            line_a, line_i = row(now_a, i), row(now_i, i)
            low_a = row(now_a, i + 1) - ratio * line_a
            low_i = row(now_i, i + 1) - ratio * line_i
            now_a = now_a - scale * line_a - second * low_a
            now_i = now_i - scale * line_i - second * low_i
            next_a = next_a + (scale_next * line_a + second_next * low_a)
            next_i = next_i + (scale_next * line_i + second_next * low_i)
        finished = jnp.concatenate([now_a * norm, now_i * norm], axis=1)
        done[pl.ds(at, STRIP), :] = finished
        ahead = work[pl.ds(at + STRIP, STRIP), :]
        return (ahead - jnp.concatenate([next_a, next_i], axis=1), finished)

    first = work[0:STRIP, :]
    lax.fori_loop(0, rows // STRIP, strip, (first, jnp.zeros_like(first)))


def solve_rows(wide, solve_high, solve_low):
    half = solve_high.shape[0] // 2
    high, low = halves(wide[...])
    left = product3(
        (high[:, :half], low[:, :half]),
        (solve_high[:half, :half], solve_low[:half, :half]),
        NT,
    )
    right = product3((high, low), (solve_high[half:, :], solve_low[half:, :]), NT)
    return jnp.concatenate([left, right], axis=1)


def update_kernel(dims, meta, front, owner, reduced, *refs):
    pts_count, grp_count, quarter, clusters, ring = dims
    first, swapped, second, third, fourth, kept_chunk = refs[:6]
    refs = refs[6:]
    count = first.shape[0]
    chunk = BAND * quarter
    crossed = (second, third, fourth)
    sides = [(first, 0)] + [(ref, 0) for ref in crossed]
    sides += [(swapped, 0)] + [(ref, count) for ref in crossed]
    chunks = (
        (kept_chunk, 0), (swapped, count), (second, 2 * count), (second, 2 * count + chunk)
    )
    tail, solve_high, solve_low, behind_high, behind_low = refs[:5]
    tiles_out, rhs_out, panel_out, wide, ahead_high, ahead_low, gathered = refs[5:]
    rows = tiles_out.shape[1]
    residue, my_grp, start = residue_of(owner, meta, pts_count), meta[1], front[0]
    device = meta[2]
    stride = pts_count // BAND
    gather(gathered, sides, meta, clusters, ring)
    for j in range(FRONT):
        if j:
            clear = jnp.zeros((j * rows, rows), jnp.float32)
            wide[0 : j * rows, j * rows : (j + 1) * rows] = clear
        for i in range(j, BEFORE):
            e = BEFORE + j - i
            home = lax.rem(start + j + clusters - e, clusters)
            tile = fetch(
                gathered, owner, BAND * home + e, j // stride, (pts_count, grp_count, quarter)
            )
            wide[i * rows : (i + 1) * rows, j * rows : (j + 1) * rows] = tile
    result = solve_rows(wide, solve_high, solve_low)
    wide[...] = result
    high, low = halves(result)
    ahead_high[...] = high
    ahead_low[...] = low
    first = pl.ds(pl.multiple_of(my_grp * rows, rows), rows)
    panel_out[0 : BEFORE * rows, :] = wide[:, first]
    panel_out[BEFORE * rows :, :] = tail[0 : (BEFORE + FRONT) * rows, :]
    base = start + clusters - BEFORE

    def ahead(position):
        at = pl.ds(pl.multiple_of(position * rows, rows), rows)
        return (ahead_high[at, :], ahead_low[at, :])

    def past(position):
        at = pl.ds(pl.multiple_of((position - BEFORE - FRONT) * rows, rows), rows)
        return (behind_high[at, :], behind_low[at, :])

    def is_ahead(position):
        return position < BEFORE

    def is_past(position):
        return (position < WINDOW) & (position >= BEFORE + FRONT)

    for i in range(BAND):
        tile = residue + pts_count * (BAND * my_grp + i)
        home = tile // BAND
        offset = lax.rem(tile, BAND)
        one = lax.rem(home + 2 * clusters - base, clusters)
        two = lax.rem(home + offset + 2 * clusters - base, clusters)
        for bit in range(grp_count):
            at = pl.multiple_of((my_grp ^ bit) * quarter, quarter)
            ref, begin = chunks[bit]
            begin = begin + i * quarter
            tiles_out[i, pl.ds(at, quarter), :] = ref[begin : begin + quarter, :]
        for left, right, test_left, test_right in (
            (ahead, ahead, is_ahead, is_ahead),
            (ahead, past, is_ahead, is_past),
            (past, past, is_past, is_past),
        ):
            @pl.when(test_left(one) & test_right(two))
            def _():
                tiles_out[i] = tiles_out[i] - product3(left(one), right(two), NT)

    position = lax.rem(device + 2 * clusters - base, clusters)
    mine = reduced[pl.ds(device, 1), :]
    rhs_out[...] = mine
    last = (BEFORE + FRONT) * rows
    front_row = [tail[last + 8 * j : last + 8 * j + 8, :] for j in range(FRONT)]
    for take, test in ((ahead, is_ahead), (past, is_past)):
        @pl.when(test(position))
        def _():
            known = halves(jnp.concatenate(front_row, axis=1))
            rhs_out[...] = mine - product3(known, take(position), NT)[0:1, :]

    @pl.when((position >= BEFORE) & (position < BEFORE + FRONT))
    def _():
        at = pl.multiple_of(last + 8 * (position - BEFORE), 8)
        rhs_out[...] = tail[pl.ds(at, 8), :][0:1, :]


def per_device(
    jacobian, point_blocks, point_grad, camera_grad, damping, incidence, tile_owner, front_first
):
    pts_count = lax.axis_size("pts")
    grp_count = lax.axis_size("grp")
    clusters = pts_count * grp_count
    my_grp = lax.axis_index("grp")
    my_pts = lax.axis_index("pts")
    device = my_pts * grp_count + my_grp
    rows = jacobian.shape[2]
    points = jacobian.shape[4]
    piece = rows // GROUP
    quarter = rows // grp_count
    capacity = (BAND * (SPAN - 1)) // pts_count + 1
    stride = pts_count // BAND
    sets = -(-FRONT // stride)
    f32 = jnp.float32
    layers = clusters // GROUP
    columns = [[GROUP * z + e for z in range(layers)] for e in range(GROUP)]
    swap = [(i, i ^ 1) for i in range(clusters)]

    def flip(values, axis, count):
        moved = [
            lax.ppermute(value, axis, [(p, p ^ (bit + 1)) for p in range(count)])
            for bit, value in enumerate(values[1:])
        ]
        return [values[0], *moved]

    def exchange(value, lists):
        return lax.all_to_all(
            value, AXES, split_axis=0, concat_axis=0, tiled=True, axis_index_groups=lists
        )

    lane = jnp.arange(8)
    meta = jnp.where(lane == 0, my_pts, jnp.where(lane == 1, my_grp, device)).astype(jnp.int32)
    bf16 = jnp.bfloat16
    jac = jnp.transpose(jacobian[0], (2, 0, 1, 3))
    block_rows = PAIRS * piece + 2 * BAND
    sent = call(
        functools.partial(pair_kernel, (rows, points, piece, grp_count, clusters)),
        [jax.ShapeDtypeStruct((block_rows, rows), f32)] * GROUP,
        (meta, incidence, jac, point_blocks[0], point_grad[0], camera_grad),
        (SM, SM, VM, VM, VM, VM),
        (
            pltpu.VMEM((GROUP, block_rows, rows), f32),
            pltpu.VMEM((TOUCH, rows, 3 * points), bf16),
            pltpu.VMEM((TOUCH * rows, 3 * points), bf16),
            pltpu.VMEM((BAND, rows), f32),
            pltpu.VMEM((16, 3 * points), bf16),
        ),
        flops=2 * PAIRS * rows * rows * 3 * points,
    )
    got = flip(sent, AXES, clusters)
    sends = pts_count if pts_count <= GROUP else 1
    send_rows = capacity * piece + BAND
    shape = (send_rows, rows) if sends > 1 else (pts_count, send_rows, rows)
    sent = call(
        functools.partial(merge_kernel, (piece, pts_count, capacity, sends)),
        [jax.ShapeDtypeStruct(shape, f32)] * sends,
        (tile_owner, meta, *got),
        (SM, SM) + (VM,) * GROUP,
        (
            pltpu.VMEM((GROUP, block_rows, rows), f32),
            pltpu.VMEM((pts_count, send_rows, rows), f32),
            pltpu.VMEM((2 * BAND, rows), f32),
            pltpu.VMEM((GROUP, rows), jnp.int32),
            pltpu.SMEM((GROUP, rows), jnp.int32),
            pltpu.SemaphoreType.DMA(()),
        ),
    )
    if sends > 1:
        got = flip(sent, "pts", pts_count)
    else:
        got = [lax.all_to_all(sent[0], "pts", split_axis=0, concat_axis=0, tiled=True)]
    copies = layers if layers > 4 else 1
    *chunks, direct, mirror, reduced = call(
        functools.partial(
            owner_kernel,
            (piece, pts_count, capacity, grp_count, quarter, clusters, sets, sends),
        ),
        [jax.ShapeDtypeStruct((BAND * quarter, rows), f32)] * grp_count
        + [
            jax.ShapeDtypeStruct((copies * sets * quarter, rows), f32),
            jax.ShapeDtypeStruct((copies * sets * quarter, rows), f32),
            jax.ShapeDtypeStruct((clusters, rows), f32),
        ],
        (tile_owner, meta, front_first, damping, *got),
        (SM, SM, SM, VM) + (VM,) * sends,
        (
            pltpu.VMEM((pts_count, send_rows, rows), f32),
            pltpu.VMEM((grp_count, BAND, quarter, rows), f32),
        ),
    )
    ring = layers <= 4

    def along(value):
        if not ring:
            return exchange(value, columns)
        moved = []
        for z in range(1, layers):
            pairs = [(p, (p + GROUP * z) % clusters) for p in range(clusters)]
            moved.append(lax.ppermute(value, AXES, pairs))
        return jnp.concatenate([value, *moved])

    def across(values):
        moved = []
        for i, value in enumerate(values):
            pairs = [(p, p ^ (2 * i + 2)) for p in range(clusters)]
            moved.append(lax.ppermute(value, AXES, pairs))
        return moved

    direct = along(direct)
    direct, mirror, *chunks = lax.optimization_barrier((direct, mirror, *chunks))
    mine = [direct, *across([direct] * 3)]
    theirs = [lax.ppermute(direct, AXES, swap)]
    mirror = along(mirror)
    swapped = lax.ppermute(jnp.concatenate([mirror, chunks[1], chunks[3]]), AXES, swap)
    count = mirror.shape[0]
    chunk = BAND * quarter
    both = jnp.concatenate([mirror, swapped[:count]])
    more = jnp.concatenate([both, chunks[2], swapped[count + chunk :]])
    both, more, mine[-1] = lax.optimization_barrier((both, more, mine[-1]))
    theirs += [lax.ppermute(x, AXES, swap) for x in mine[1:]]
    sides = [mirror, swapped, *across([more, both, both]), chunks[0]]

    width = FRONT * rows
    dims = (pts_count, grp_count, quarter, clusters)
    tall = BEFORE * rows + 8
    tail = (FRONT + BEFORE) * rows + 8 * FRONT
    shapes = (
        ((tail, rows), f32),
        ((width, width), bf16),
        ((width, width), bf16),
        ((tall, width), bf16),
        ((tall, width), bf16),
    )
    stored = call(
        functools.partial(factor_kernel, dims + (ring,)),
        [jax.ShapeDtypeStruct(*x) for x in shapes],
        (meta, front_first, tile_owner, reduced, *mine, *theirs),
        (SM, SM, SM, VM) + (VM,) * GROUP,
        [
            pltpu.VMEM((FRONT, rows, width), f32),
            pltpu.VMEM((tall, width), f32),
            pltpu.VMEM((clusters, sets * quarter, rows), f32),
            pltpu.VMEM((rows + STRIP, 2 * rows), f32),
            pltpu.VMEM((rows, 2 * rows), f32),
            pltpu.VMEM((FRONT, rows, 2 * width), f32),
            pltpu.VMEM((tall, width), f32),
        ],
        flops=400 * rows * rows * rows * 6,
    )
    return tuple(call(
        functools.partial(update_kernel, dims + (ring,)),
        [
            jax.ShapeDtypeStruct((BAND, rows, rows), f32),
            jax.ShapeDtypeStruct((1, rows), f32),
            jax.ShapeDtypeStruct((WINDOW * rows, rows), f32),
        ],
        (meta, front_first, tile_owner, reduced, *sides, *stored),
        (SM, SM, SM, VM) + (VM,) * 11,
        [
            pltpu.VMEM((BEFORE * rows, width), f32),
            pltpu.VMEM((BEFORE * rows, width), bf16),
            pltpu.VMEM((BEFORE * rows, width), bf16),
            pltpu.VMEM((clusters, sets * quarter, rows), f32),
        ],
        flops=200 * rows * rows * rows * 6,
    ))


def solution(mesh):
    in_specs = (
        P(AXES, None, None, None, None),
        P(AXES, None, None),
        P(AXES, None, None),
        P(AXES, None),
        P(),
        P(AXES, None),
        P(),
        P(),
    )
    out_specs = (P(AXES, None, None), P(AXES, None), P(None, "grp"))

    return jax.shard_map(per_device, mesh=mesh, in_specs=in_specs, out_specs=out_specs, check_vma=False)
```
